256 devices in a mesh: gx: 16 (over z, y_lo), gy: 16 (over x, y_hi, core).
Axes of the slice: x: 4, y: 4 (y_hi: 2, y_lo: 2; y = y_hi * 2 + y_lo), z: 8, core: 2. Of those that a mesh axis runs over, the one named last changes fastest.
Arguments:
- fields: float32 [4, 256, 4096], P(None, 'gx', 'gy'), may hold values from -6 to 6
- pore_mask: int32 [256, 4096], P('gx', 'gy'), may hold values 0 or 1
- collision_rate: float32 [256, 4096], P('gx', 'gy'), may hold values from 0.05 to 3
- particles: float32 [8, 256, 32768], P(None, 'gx', 'gy')
- occupancy: int32 [256, 256], P('gx', 'gy'), may hold values from 32 to 96, as said below
- slot_cell: int32 [256, 32768], P('gx', 'gy'), may hold values from 0 to 15
- send_slot: int32 [16, 16, 6144], P(None, 'gx', 'gy'), may hold values from 0 to 32767, as said below
- send_count: int32 [16, 16, 16], P(None, 'gx', 'gy'), may hold values from 4 to 384, as said below
- land_slot: int32 [16, 16, 6144], P(None, 'gx', 'gy'), may hold values from 0 to 32767, as said below
Outputs:
- fields_out: float32 [4, 256, 4096], P(None, 'gx', 'gy')
- particles_out: float32 [8, 256, 32768], P(None, 'gx', 'gy')
The draws below stay inside these ranges and needn't reach their ends.
Inputs may be any that keep to these rules, and one draw needn't show every extreme that they name: `send_count`: for directions 0 to 3 every count lies between 128 and 384, for directions 4 to 7 between 4 and 16; for every step and direction some device's count is exactly that direction's most. `occupancy`: every block has between 32 and 96 live slots, both ends reached. `send_slot`: entries are slot indices b * 128 + j of the device's own blocks; all entries of one device, over both steps and all directions, are distinct live slots. `land_slot`: entries are slot indices b * 128 + j of the device's own blocks; all entries of one device are distinct slots that are not live at the start.
All inputs are finite; a program needn't handle non-finite values. No bound on the sum of `pore_mask` on one device may be relied on, other than what follows from the above.
Results may differ from the reference program's by a relative error of at most 0.0003.
Values sent between devices are 32-bit elements; how exact they have to be, the bound alone decides.
A program may use at most 256 MiB of HBM per device.

```python
import math
import jax
import jax.numpy as jnp
from jax import lax

CX = 16
CY = 16
CZ = 16
SLOTS = 128
STEPS = 2
CAP = 384
CAP_DIAG = 16
NX = 256
NY = 256
N_GX = 16
N_GY = 16


def occupancy_table(key):
    base = jax.random.fold_in(key, 11)
    table = jax.random.randint(base, (NX * NY,), SLOTS // 4, 3 * SLOTS // 4 + 1)
    spots = jax.random.randint(jax.random.fold_in(key, 15), (2,), 0, NX * NY)
    places = jnp.arange(NX * NY)
    table = jnp.where(places == spots[0], 3 * SLOTS // 4, table)
    table = jnp.where((places == spots[1]) & (places != spots[0]), SLOTS // 4, table)
    return table.reshape(NX, NY).astype(jnp.int32)


def device_lists(dev_key, occ_dev):
    total = CX * CY * SLOTS
    need = 16 * CAP
    live = (jnp.arange(SLOTS)[None, :] < occ_dev[:, None]).reshape(-1)
    perm = jax.random.permutation(dev_key, total)
    rank_key = jnp.where(live[perm], 0, 1)
    order = jnp.argsort(rank_key, stable=True)
    ranked = perm[order].astype(jnp.int32)
    return (ranked[:need].reshape(16, CAP), ranked[total - need:].reshape(16, CAP))


def slot_lists(key):
    grid_x = NX // CX
    grid_y = NY // CY
    occ = occupancy_table(key)
    occ_dev = occ.reshape(grid_x, CX, grid_y, CY).transpose(0, 2, 1, 3).reshape(grid_x * grid_y, CX * CY)
    keys = jax.random.split(jax.random.fold_in(key, 12), grid_x * grid_y)
    sends, lands = jax.vmap(device_lists)(keys, occ_dev)

    def arrange(arr):
        return arr.reshape(grid_x, grid_y, 16, CAP).transpose(2, 0, 1, 3).reshape(16, grid_x, grid_y * CAP)
    return (arrange(sends), arrange(lands))


def draw_occupancy(key, part):
    return occupancy_table(key)


def draw_send_slot(key, part):
    return slot_lists(key)[0]


def draw_land_slot(key, part):
    return slot_lists(key)[1]


def draw_send_count(key, part):
    grid_x = NX // CX
    grid_y = NY // CY
    tiles = grid_x * grid_y
    axial = jax.random.randint(jax.random.fold_in(key, 13), (16, tiles), CAP // 3, CAP + 1)
    corner = jax.random.randint(jax.random.fold_in(key, 16), (16, tiles), CAP_DIAG // 4, CAP_DIAG + 1)
    is_corner = (jnp.arange(16) % 8 >= 4)[:, None]
    base = jnp.where(is_corner, corner, axial)
    most = jnp.where(is_corner, CAP_DIAG, CAP)
    spots = jax.random.randint(jax.random.fold_in(key, 14), (16, 1), 0, tiles)
    counts = jnp.where(jnp.arange(tiles)[None, :] == spots, most, base)
    return counts.reshape(16, grid_x, grid_y).astype(jnp.int32)


def draw_particles(key, part):
    shape = (NX, NY * SLOTS)
    keys = jax.random.split(jax.random.fold_in(key, 21), 4)
    position = jax.random.uniform(keys[0], (3,) + shape, jnp.float32, 0.0, 1.0)
    velocity = jax.random.normal(keys[1], (3,) + shape, jnp.float32)
    weight = jnp.exp(jax.random.uniform(keys[2], (1,) + shape, jnp.float32, -2.3, 0.0))
    rotation = jax.random.uniform(keys[3], (1,) + shape, jnp.float32, 0.2, 2.0)
    return jnp.concatenate([position, velocity, weight, rotation], axis=0).astype(jnp.float32)


def set_ends(entries, own_key, smallest, top_value):
    spot = [jax.random.randint(jax.random.fold_in(own_key, axis), (), 0, length) for axis, length in enumerate(entries.shape)]
    widest = entries.shape.index(max(entries.shape))
    beside = spot[:widest] + [(spot[widest] + 1) % entries.shape[widest]] + spot[widest + 1:]
    return entries.at[tuple(spot)].set(smallest).at[tuple(beside)].set(top_value)


def block_levels(key, shape, shards, least, top_value):
    def one(dim, parts):
        steps = jax.random.uniform(jax.random.fold_in(jax.random.fold_in(key, 6), dim), (parts,), jnp.float32, least / len(shards), top_value / len(shards))
        return jnp.repeat(jnp.exp(steps), shape[dim] // parts).reshape((-1,) + (1,) * (len(shape) - dim - 1))

    factor_of = one(*shards[0])
    for cut in shards[1:]:
        factor_of = factor_of * one(*cut)
    return factor_of


def bell_draw(rng, shape, deviation, most, cuts=(), held_as=jnp.bfloat16):
    drawn = deviation * jax.random.normal(rng, shape, jnp.float32)
    if cuts:
        drawn = drawn * block_levels(rng, shape, cuts, -0.22, 0.18)
    return jnp.clip(drawn, -most, most).astype(held_as)


def setup_inputs(seed: int = 0) -> dict:
    key_list = jax.random.split(jax.random.key(seed), 10)
    fields = bell_draw(key_list[0], (4, NX, NY * CZ), 1.0, 6.0, ((1, 16), (2, 16)), jnp.float32)
    pore_mask = set_ends((jax.random.randint(key_list[1], (NX, NY * CZ), 0, 4) < 3).astype(jnp.int32), jax.random.fold_in(key_list[1], 1), 0, 1)
    collision_rate = jnp.clip(jnp.exp(math.log(3.0) - 4.0943445 * jax.random.uniform(key_list[2], (NX, NY * CZ), jnp.float32) ** block_levels(key_list[2], (NX, NY * CZ), ((0, 16), (1, 16)), -0.2, 0.2)), 0.05, 3.0)
    particles = draw_particles(jax.random.fold_in(key_list[9], 71), 0)
    occupancy = draw_occupancy(jax.random.fold_in(key_list[9], 71), 0)
    slot_cell = set_ends(jax.random.randint(key_list[5], (NX, NY * SLOTS), 0, CZ), jax.random.fold_in(key_list[5], 1), 0, CZ - 1).astype(jnp.int32)
    send_slot = draw_send_slot(jax.random.fold_in(key_list[9], 71), 0)
    send_count = draw_send_count(jax.random.fold_in(key_list[9], 71), 0)
    land_slot = draw_land_slot(jax.random.fold_in(key_list[9], 71), 0)
    return {"fields": fields, "pore_mask": pore_mask, "collision_rate": collision_rate, "particles": particles, "occupancy": occupancy, "slot_cell": slot_cell, "send_slot": send_slot, "send_count": send_count, "land_slot": land_slot}


courant = 0.25
rot_number = 4.0


def normal_flux(state, axis_n):
    rho = state[0]
    zero = jnp.zeros_like(rho)
    comps = [state[1 + axis_n], zero, zero, zero]
    comps[1 + axis_n] = rho
    return jnp.stack(comps)


def face_flux(far_left, left, right, far_right, coef, axis_n):
    centred = (7.0 / 12.0) * (normal_flux(left, axis_n) + normal_flux(right, axis_n)) - (1.0 / 12.0) * (normal_flux(far_left, axis_n) + normal_flux(far_right, axis_n))
    return coef[None] * (centred - 0.5 * (right - left))


def face_coef(mask_left, mask_right, keep_left, keep_right):
    return mask_left * mask_right * (1.0 - 0.5 * (keep_left + keep_right))


def divergence(total, fluid, keep):
    padded = jnp.pad(total, ((0, 0), (2, 2), (2, 2), (2, 2)))
    pad_mask = jnp.pad(fluid, 2)
    pad_keep = jnp.pad(keep, 2)
    result = jnp.zeros_like(total)
    for axis_n in range(3):
        count = total.shape[1 + axis_n]

        def cut(arr, start, lead):
            index = [slice(2, -2), slice(2, -2), slice(2, -2)]
            index[axis_n] = slice(start, start + count + 1)
            return arr[tuple([slice(None)] * lead + index)]

        coef = face_coef(cut(pad_mask, 1, 0), cut(pad_mask, 2, 0), cut(pad_keep, 1, 0), cut(pad_keep, 2, 0))
        flux = face_flux(cut(padded, 0, 1), cut(padded, 1, 1), cut(padded, 2, 1), cut(padded, 3, 1), coef, axis_n)
        upper = lax.slice_in_dim(flux, 1, count + 1, axis=1 + axis_n)
        lower = lax.slice_in_dim(flux, 0, count, axis=1 + axis_n)
        result = result + (upper - lower)
    return result


def deposit(state, cell_of, cells):
    weight = state[6]
    values = jnp.stack([weight, weight * state[3], weight * state[4], weight * state[5]])
    return jax.vmap(lambda v: jax.ops.segment_sum(v, cell_of, num_segments=cells))(values)


def collide(state, keep_slot, rate_slot):
    position = state[0:3] + courant * state[3:6]
    weight = state[6] * keep_slot
    rotation = 1.0 + (state[7] - 1.0) * jnp.exp(-rate_slot / rot_number)
    return jnp.concatenate([position, state[3:6], weight[None], rotation[None]], axis=0)


def reference(fields, pore_mask, collision_rate, particles, occupancy, slot_cell, send_slot, send_count, land_slot):
    grid_x = N_GX
    grid_y = N_GY
    slots_all = CX * CY * SLOTS
    cells = CX * CY * CZ

    def to_dev(arr, comps, inner):
        shaped = arr.reshape(comps, grid_x, CX, grid_y, inner)
        return shaped.transpose(1, 3, 0, 2, 4).reshape(grid_x, grid_y, comps, CX * inner)

    def from_dev(arr, comps, inner):
        shaped = arr.reshape(grid_x, grid_y, comps, CX, inner)
        return shaped.transpose(2, 0, 3, 1, 4).reshape(comps, grid_x * CX, grid_y * inner)

    def shift_tiles(arr, step_x, step_y):
        widths = [(1, 1), (1, 1)] + [(0, 0)] * (arr.ndim - 2)
        padded = jnp.pad(arr, widths)
        return padded[1 - step_x:1 - step_x + grid_x, 1 - step_y:1 - step_y + grid_y]

    fluid = pore_mask.astype(jnp.float32)
    keep = jnp.exp(-collision_rate)
    fluid_grid = fluid.reshape(NX, NY, CZ)
    keep_grid = keep.reshape(NX, NY, CZ)
    state = to_dev(particles, 8, CY * SLOTS)
    occ = to_dev(occupancy[None], 1, CY)[:, :, 0]
    slot_z = to_dev(slot_cell[None], 1, CY * SLOTS)[:, :, 0]
    keep_dev = to_dev(keep[None], 1, CY * CZ)[:, :, 0]
    rate_dev = to_dev(collision_rate[None], 1, CY * CZ)[:, :, 0]
    sends = send_slot.reshape(STEPS * 8, grid_x, grid_y, CAP).transpose(1, 2, 0, 3).reshape(grid_x, grid_y, STEPS, 8, CAP)
    lands = land_slot.reshape(STEPS * 8, grid_x, grid_y, CAP).transpose(1, 2, 0, 3).reshape(grid_x, grid_y, STEPS, 8, CAP)
    counts = send_count.transpose(1, 2, 0).reshape(grid_x, grid_y, STEPS, 8)

    slot_pos = jnp.arange(slots_all, dtype=jnp.int32)
    block = (slot_pos // SLOTS).astype(jnp.int32)
    live = ((slot_pos % SLOTS)[None, None, :] < jnp.take(occ, block, axis=2)).astype(jnp.float32)
    state = state * live[:, :, None, :]
    cell_of = (block[None, None, :] * CZ + slot_z).astype(jnp.int32)
    keep_slot = jax.vmap(jax.vmap(lambda table, idx: table[idx]))(keep_dev, cell_of)
    rate_slot = jax.vmap(jax.vmap(lambda table, idx: table[idx]))(rate_dev, cell_of)
    lane = jnp.arange(CAP, dtype=jnp.int32)
    moves = [(1, 0), (-1, 0), (0, 1), (0, -1), (1, 1), (1, -1), (-1, 1), (-1, -1)]
    dev_map = lambda fn: jax.vmap(jax.vmap(fn))

    for step in range(STEPS):
        moments_dev = dev_map(lambda s, c: deposit(s, c, cells))(state, cell_of)
        moments = from_dev(moments_dev, 4, CY * CZ)
        total = (fields + moments) * fluid[None]
        div = divergence(total.reshape(4, NX, NY, CZ), fluid_grid, keep_grid).reshape(4, NX, NY * CZ)
        fields = fields - courant * div + (1.0 - keep)[None] * moments
        state = dev_map(collide)(state, keep_slot, rate_slot)
        valid = lane[None, None, None, :] < counts[:, :, step][..., None]
        send_now = sends[:, :, step]
        outgoing = dev_map(lambda s, idx: jnp.take(s, idx, axis=1))(state, send_now) * valid[:, :, None]
        gone = jnp.where(valid, send_now, slots_all).astype(jnp.int32)
        state = dev_map(lambda s, idx: s.at[:, idx.reshape(-1)].set(0.0, mode="drop"))(state, gone)
        arriving = []
        arrived_n = []
        for direction in range(8):
            step_x, step_y = moves[direction]
            arriving.append(shift_tiles(outgoing[:, :, :, direction], step_x, step_y))
            arrived_n.append(shift_tiles(counts[:, :, step, direction], step_x, step_y))
        arriving = jnp.stack(arriving, axis=3)
        arrived_n = jnp.stack(arrived_n, axis=2)
        fit = lane[None, None, None, :] < arrived_n[..., None]
        target = jnp.where(fit, lands[:, :, step], slots_all).astype(jnp.int32)
        state = dev_map(lambda s, idx, rows: s.at[:, idx.reshape(-1)].set(rows.reshape(8, -1), mode="drop"))(state, target, arriving)
    return fields, from_dev(state, 8, CY * SLOTS)
```

```python
import jax
import jax.numpy as jnp
from jax import lax
from jax.experimental import pallas as pl
from jax.experimental.pallas import tpu as pltpu
from jax.sharding import PartitionSpec as P

CX = 16
CY = 16
CZ = 16
SLOTS = 128
STEPS = 2
CAP = 384
DIAG = 16
BLOCKS = CX * CY
FLAT = CY * CZ
AXIAL = 4 * CAP
LIST = AXIAL + 128
COURANT = 0.25
ROT = 4.0
MOVES = ((1, 0), (-1, 0), (0, 1), (0, -1), (1, 1), (1, -1), (-1, 1), (-1, -1))
F32 = jnp.float32
BF16 = jnp.bfloat16
I32 = jnp.int32
MESH = pl.DeviceIdType.MESH


def iota(shape, dim):
    return lax.broadcasted_iota(I32, shape, dim)


def split(x):
    high = (x * 0.995).astype(BF16)
    low = (x - high.astype(F32)).astype(BF16)
    return high, low


def dot(a, b):
    return lax.dot_general(a, b, (((1,), (0,)), ((), ())), preferred_element_type=F32)


def dot_nt(a, b):
    return lax.dot_general(a, b, (((1,), (1,)), ((), ())), preferred_element_type=F32)


def roll(x, by, axis):
    return pltpu.roll(x, by % x.shape[axis], axis)


def onehot_rows(row, size):
    n = row.shape[1]
    return jnp.where(iota((size, n), 0) == row, 1.0, 0.0).astype(BF16)


def block_row(slot):
    block = slot >> 7
    return (block & 15) * CX + (block >> 4)


def flux_of(comps, coef, axis_n, move):
    nxt = [move(w, 1) for w in comps]

    def centred(w, w_next):
        return 7.0 / 12.0 * (w + w_next) - 1.0 / 12.0 * (move(w, -1) + move(w, 2))

    out = []
    for c in range(4):
        value = -0.5 * (nxt[c] - comps[c])
        if c == 0:
            value = value + centred(comps[1 + axis_n], nxt[1 + axis_n])
        if c == 1 + axis_n:
            value = value + centred(comps[0], nxt[0])
        out.append(coef * value)
    return out


def kernel(
    nx,
    ny,
    fields_ref,
    pore_ref,
    rate_ref,
    part_ref,
    occ_ref,
    cell_ref,
    send_ref,
    count_ref,
    land_ref,
    fields_out,
    part_out,
    state,
    split_state,
    values,
    deposit_hot,
    total,
    fk,
    fkx,
    fky,
    hx,
    hy,
    axial_out,
    axial_in,
    diag_out,
    diag_in,
    send_sem,
    recv_sem,
):
    ix = lax.axis_index("gx")
    iy = lax.axis_index("gy")

    def device(move):
        return (lax.rem(ix + move[0] + nx, nx), lax.rem(iy + move[1] + ny, ny))

    def present(move):
        x, y = ix - move[0], iy - move[1]
        return (x >= 0) & (x < nx) & (y >= 0) & (y < ny)

    copies = []

    def send(src, dst, move):
        k = len(copies)
        copy = pltpu.make_async_remote_copy(
            src_ref=src,
            dst_ref=dst,
            send_sem=send_sem.at[k],
            recv_sem=recv_sem.at[k],
            device_id=device(move),
            device_id_type=MESH,
        )
        copy.start()
        copies.append(copy)
        return copy

    barrier = pltpu.get_barrier_semaphore()
    for move in MOVES:
        pl.semaphore_signal(barrier, inc=1, device_id=device(move), device_id_type=MESH)

    def lanes_of(y):
        return slice(y * SLOTS, (y + 1) * SLOTS)

    def rows_of(y):
        return slice(y * CX, (y + 1) * CX)

    rate = rate_ref[...]
    keep = jnp.exp(-rate)
    relax = jnp.exp(-rate / ROT)
    fluid = pore_ref[...].astype(F32)
    fk[0] = fluid
    fk[1] = keep
    lane = iota((CX, SLOTS), 1)

    keep_slot, relax_slot = [], []
    for y in range(CY):
        half = slice((y // 8) * 128, (y // 8) * 128 + 128)
        index = cell_ref[:, lanes_of(y)] + (y % 8) * CZ
        keep_slot.append(jnp.take_along_axis(keep[:, half], index, axis=1))
        relax_slot.append(jnp.take_along_axis(relax[:, half], index, axis=1))

    occ = occ_ref[...]
    for y in range(CY):
        live = lane < occ[:, y : y + 1]
        for c in range(8):
            state[c, rows_of(y), :] = jnp.where(live, part_ref[c, :, lanes_of(y)], 0.0)

    def put_split(c, y, value):
        high, low = split(value)
        split_state[c * BLOCKS + y * CX : c * BLOCKS + (y + 1) * CX, 0:128] = high
        split_state[c * BLOCKS + y * CX : c * BLOCKS + (y + 1) * CX, 128:256] = low

    def send_list(step):
        slots, used = [], []
        for d in range(4):
            slots.append(send_ref[step * 8 + d])
            used.append(iota((1, CAP), 1) < count_ref[step * 8 + d])
        corner = diag_rows(send_ref, step)
        at = iota((1, 128), 1)
        ok = at < 0
        for d in range(4):
            ok = ok | ((at >= d * DIAG) & (at < d * DIAG + count_ref[step * 8 + 4 + d]))
        slots.append(corner)
        used.append(ok)
        return jnp.concatenate(slots, axis=1), [u.astype(I32) for u in used]

    def diag_rows(ref, step):
        at = iota((8, 128), 1) // DIAG
        out = jnp.zeros((8, 128), I32)
        for d in range(4):
            row = jnp.broadcast_to(ref[step * 8 + 4 + d][:, 0:128], (8, 128))
            out = jnp.where(at == d, roll(row, d * DIAG, 1), out)
        return out[0:1]

    def gather(step):
        slots, used = send_list(step)
        ok = jnp.concatenate(used, axis=1) > 0
        row = jnp.where(ok, block_row(slots), -1)
        place = slots & 127
        hot = []
        for start in range(0, LIST, 256):
            stop = min(start + 256, LIST)
            n = stop - start
            place_hot = onehot_rows(place[:, start:stop], SLOTS)
            hot.append(place_hot)
            mine = iota((BLOCKS, n), 0) == row[:, start:stop]
            product = dot(split_state[...], jnp.concatenate([place_hot, place_hot], axis=0))
            got = [
                jnp.sum(
                    jnp.where(mine, product[c * BLOCKS : (c + 1) * BLOCKS], 0.0),
                    axis=0,
                    keepdims=True,
                )
                for c in range(8)
            ]
            got = jnp.concatenate(got, axis=0)
            for tile in range(start // 128, stop // 128):
                piece = got[:, tile * 128 - start : tile * 128 - start + 128]
                if tile < AXIAL // 128:
                    at = (tile % 3) * 128
                    axial_out[step, tile // 3, :, at : at + 128] = piece
                else:
                    flag = jnp.broadcast_to(used[4].astype(F32), (8, 128))
                    diag_out[step] = jnp.where(
                        iota((8, 128), 1) < 64, piece, roll(flag, 64, 1)
                    )
        for d in range(4):
            axial_out[step, d, :, CAP : CAP + 128] = jnp.full(
                (8, 128), count_ref[step * 8 + d].astype(F32), F32
            )
        return row, jnp.concatenate(hot, axis=1)

    def send_particles(step):
        mine = []
        for d in range(4):
            mine.append(send(axial_out.at[step, d], axial_in.at[step, d], MOVES[d]))
        for d in range(4):
            mine.append(send(diag_out.at[step], diag_in.at[step, d], MOVES[4 + d]))
        return mine

    def deposit():
        for y in range(CY):
            w = state[6, rows_of(y), :]
            values[0, rows_of(y), :] = w
            for c in range(3):
                values[1 + c, rows_of(y), :] = w * state[3 + c, rows_of(y), :]
        own = iota((CY, FLAT), 1) // CZ == iota((CY, FLAT), 0)
        out = [[] for _ in range(4)]
        for x in range(CX):
            picked = jnp.concatenate(
                [values[c, pl.ds(x, CY, stride=CX), :] for c in range(4)], axis=0
            )
            high, low = split(picked)
            both = dot_nt(jnp.concatenate([high, low], axis=0), deposit_hot[x])
            both = both[: 4 * CY] + both[4 * CY :]
            for c in range(4):
                part = jnp.where(own, both[c * CY : (c + 1) * CY], 0.0)
                out[c].append(jnp.sum(part, axis=0, keepdims=True))
        return [jnp.concatenate(o, axis=0) for o in out]

    def send_halo(step):
        return [
            send(total.at[step, :, 8:16, :], hx.at[step, 0], MOVES[0]),
            send(total.at[step, :, 0:8, :], hx.at[step, 1], MOVES[1]),
            send(total.at[step, :, :, 128:256], hy.at[step, 0], MOVES[2]),
            send(total.at[step, :, :, 0:128], hy.at[step, 1], MOVES[3]),
        ]

    def ring_x(own, low, high):
        at = iota((8, FLAT), 0)
        low = jnp.where((at >= 6) & present(MOVES[0]), low, 0.0)
        edge = jnp.where((at < 2) & present(MOVES[1]), high, low)
        return jnp.concatenate([own, edge], axis=0)

    def ring_y(own, low, high):
        at = iota((CX, 128), 1)
        low = jnp.where((at >= 96) & present(MOVES[2]), low, 0.0)
        edge = jnp.where((at < 32) & present(MOVES[3]), high, low)
        return jnp.concatenate([own, edge], axis=1)

    def move_x(w, k):
        return roll(w, -k, 0)

    def move_y(w, k):
        return roll(w, -k * CZ, 1)

    zpos = iota((CX, FLAT), 1) % CZ

    def move_z(w, k):
        inside = (zpos + k >= 0) & (zpos + k < CZ)
        return jnp.where(inside, roll(w, -k, 1), 0.0)

    def coefs():
        def one(f, k, move):
            return f * move(f, 1) * (1.0 - 0.5 * (k + move(k, 1)))

        x = one(ring_x(fluid, fkx[0, 0], fkx[1, 0]), ring_x(keep, fkx[0, 1], fkx[1, 1]), move_x)
        y = one(ring_y(fluid, fky[0, 0], fky[1, 0]), ring_y(keep, fky[0, 1], fky[1, 1]), move_y)
        return x, y, one(fluid, keep, move_z)

    def divergence(step, coef):
        own = [total[step, c] for c in range(4)]
        xs = [ring_x(own[c], hx[step, 0, c], hx[step, 1, c]) for c in range(4)]
        ys = [ring_y(own[c], hy[step, 0, c], hy[step, 1, c]) for c in range(4)]
        fx = flux_of(xs, coef[0], 0, move_x)
        fy = flux_of(ys, coef[1], 1, move_y)
        fz = flux_of(own, coef[2], 2, move_z)
        out = []
        for c in range(4):
            dx = (fx[c] - move_x(fx[c], -1))[:CX]
            dy = (fy[c] - move_y(fy[c], -1))[:, :FLAT]
            out.append(dx + dy + (fz[c] - move_z(fz[c], -1)))
        return out

    def collide(c, y, value):
        rows = rows_of(y)
        if c < 3:
            return value + COURANT * state[3 + c, rows, :]
        if c == 6:
            return value * keep_slot[y]
        return 1.0 + (value - 1.0) * relax_slot[y]

    def land_list(step):
        rows, places, parts = [], [], []
        at = iota((1, CAP), 1)
        for d in range(4):
            got = axial_in[step, d]
            fit = at.astype(F32) < jnp.broadcast_to(got[0:1, CAP : CAP + 1], (1, CAP))
            fit = fit & present(MOVES[d])
            slot = land_ref[step * 8 + d]
            rows.append(jnp.where(fit, block_row(slot), -1))
            places.append(slot & 127)
            parts.append(jnp.where(jnp.broadcast_to(fit.astype(F32), (8, CAP)) > 0, got[:, :CAP], 0.0))
        at = iota((8, 128), 1)
        got = jnp.zeros((8, 128), F32)
        for d in range(4):
            mine = (at % 64) // DIAG == d
            got = jnp.where(mine & present(MOVES[4 + d]), diag_in[step, d], got)
        fit = (roll(got, 64, 1) > 0.5) & (at < 64)
        slot = diag_rows(land_ref, step)
        rows.append(jnp.where(fit, block_row(jnp.broadcast_to(slot, (8, 128))), -1)[0:1])
        places.append(slot & 127)
        parts.append(jnp.where(fit, got, 0.0))
        return (
            jnp.concatenate(parts, axis=1),
            jnp.concatenate(rows, axis=1),
            jnp.concatenate(places, axis=1),
        )

    def land(comps, arrived, row_hot, place_hot):
        out = []
        for first in range(0, len(comps), 2):
            highs, lows = [], []
            for c in comps[first : first + 2]:
                high, low = split(arrived[c : c + 1])
                highs.append(place_hot * high)
                lows.append(place_hot * low)
            got = dot_nt(row_hot, jnp.concatenate(highs, axis=0)) + dot_nt(
                row_hot, jnp.concatenate(lows, axis=0)
            )
            out += [got[:, :128], got[:, 128:]]
        return out

    for y in range(CY):
        for c in (0, 1, 2, 6, 7):
            put_split(c, y, collide(c, y, state[c, rows_of(y), :]))
        for c in (3, 4, 5):
            put_split(c, y, state[c, rows_of(y), :])
    sent = [gather(0)]

    pl.semaphore_wait(barrier, len(MOVES))
    edges = [
        send(fk.at[:, 8:16, :], fkx.at[0], MOVES[0]),
        send(fk.at[:, 0:8, :], fkx.at[1], MOVES[1]),
        send(fk.at[:, :, 128:256], fky.at[0], MOVES[2]),
        send(fk.at[:, :, 0:128], fky.at[1], MOVES[3]),
    ]
    arrivals = [send_particles(0)]

    for x in range(CX):
        for y in range(CY):
            mine = iota((CZ, SLOTS), 0) == jnp.broadcast_to(
                cell_ref[x : x + 1, lanes_of(y)], (CZ, SLOTS)
            )
            deposit_hot[x, y * CZ : (y + 1) * CZ, :] = jnp.where(mine, 1.0, 0.0).astype(BF16)
    moments = deposit()
    for c in range(4):
        total[0, c] = (fields_ref[c] + moments[c]) * fluid
    halos = [send_halo(0)]

    for y in range(CY):
        for c in (0, 1, 2, 6, 7):
            value = collide(c, y, state[c, rows_of(y), :])
            state[c, rows_of(y), :] = value
            put_split(c, y, collide(c, y, value))
    sent.append(gather(1))
    arrivals.append(send_particles(1))

    for copy in edges + halos[0]:
        copy.wait()
    coef = coefs()
    div = divergence(0, coef)
    fields = [
        fields_ref[c] - COURANT * div[c] + (1.0 - keep) * moments[c] for c in range(4)
    ]

    everything = tuple(range(8))
    for step in range(STEPS):
        for copy in arrivals[step]:
            copy.wait()
        arrived, row, place = land_list(step)
        row_hot = onehot_rows(row, BLOCKS)
        place_hot = onehot_rows(place, SLOTS)
        sent_row, sent_place = sent[step]
        cleared = (dot_nt(row_hot, place_hot) + dot_nt(onehot_rows(sent_row, BLOCKS), sent_place)) > 0.5

        def settle(comps):
            news = land(comps, arrived, row_hot, place_hot)
            for c, new in zip(comps, news):
                state[c] = jnp.where(cleared, 0.0, state[c]) + new

        if step == 0:
            settle((6, 3, 4, 5))
            moments = deposit()
            for c in range(4):
                total[1, c] = (fields[c] + moments[c]) * fluid
            halos.append(send_halo(1))
            settle((0, 1, 2, 7))
            for y in range(CY):
                for c in (0, 1, 2, 6, 7):
                    state[c, rows_of(y), :] = collide(c, y, state[c, rows_of(y), :])
        else:
            settle(everything)

    for y in range(CY):
        for c in range(8):
            part_out[c, :, lanes_of(y)] = state[c, rows_of(y), :]
    for copy in halos[1]:
        copy.wait()
    div = divergence(1, coef)
    for c in range(4):
        fields_out[c] = fields[c] - COURANT * div[c] + (1.0 - keep) * moments[c]


def solution(mesh):
    nx, ny = mesh.shape["gx"], mesh.shape["gy"]

    def body(fields, pore, rate, particles, occupancy, slot_cell, send_slot, send_count, land_slot):
        vmem = pl.BlockSpec(memory_space=pltpu.VMEM)
        smem = pl.BlockSpec(memory_space=pltpu.SMEM)
        copies = 4 + 8 * STEPS + 4 * STEPS

        def run(*refs):
            kernel(nx, ny, *refs)

        return pl.pallas_call(
            run,
            out_shape=(
                jax.ShapeDtypeStruct(fields.shape, F32),
                jax.ShapeDtypeStruct(particles.shape, F32),
            ),
            in_specs=[vmem] * 7 + [smem, vmem],
            out_specs=(vmem, vmem),
            scratch_shapes=[
                pltpu.VMEM((8, BLOCKS, SLOTS), F32),
                pltpu.VMEM((8 * BLOCKS, 2 * SLOTS), BF16),
                pltpu.VMEM((4, BLOCKS, SLOTS), F32),
                pltpu.VMEM((CX, FLAT, SLOTS), BF16),
                pltpu.VMEM((STEPS, 4, CX, FLAT), F32),
                pltpu.VMEM((2, CX, FLAT), F32),
                pltpu.VMEM((2, 2, 8, FLAT), F32),
                pltpu.VMEM((2, 2, CX, 128), F32),
                pltpu.VMEM((STEPS, 2, 4, 8, FLAT), F32),
                pltpu.VMEM((STEPS, 2, 4, CX, 128), F32),
                pltpu.VMEM((STEPS, 4, 8, CAP + 128), F32),
                pltpu.VMEM((STEPS, 4, 8, CAP + 128), F32),
                pltpu.VMEM((STEPS, 8, 128), F32),
                pltpu.VMEM((STEPS, 4, 8, 128), F32),
                pltpu.SemaphoreType.DMA((copies,)),
                pltpu.SemaphoreType.DMA((copies,)),
            ],
            compiler_params=pltpu.CompilerParams(
                collective_id=0, has_side_effects=True, vmem_limit_bytes=48 << 20
            ),
        )(
            fields,
            pore,
            rate,
            particles,
            occupancy,
            slot_cell,
            send_slot,
            send_count.reshape(STEPS * 8),
            land_slot,
        )

    return jax.shard_map(
        body,
        mesh=mesh,
        in_specs=(
            P(None, "gx", "gy"),
            P("gx", "gy"),
            P("gx", "gy"),
            P(None, "gx", "gy"),
            P("gx", "gy"),
            P("gx", "gy"),
            P(None, "gx", "gy"),
            P(None, "gx", "gy"),
            P(None, "gx", "gy"),
        ),
        out_specs=(P(None, "gx", "gy"), P(None, "gx", "gy")),
        check_vma=False,
    )
```

```python
import jax
import jax.numpy as jnp
from jax import lax
from jax.experimental import pallas as pl
from jax.experimental.pallas import tpu as pltpu
from jax.sharding import PartitionSpec as P

CX = 16
CY = 16
CZ = 16
SLOTS = 128
STEPS = 2
CAP = 384
DIAG = 16
BLOCKS = CX * CY
FLAT = CY * CZ
AXIAL = 4 * CAP
LIST = AXIAL + 128
COURANT = 0.25
ROT = 4.0
MOVES = ((1, 0), (-1, 0), (0, 1), (0, -1), (1, 1), (1, -1), (-1, 1), (-1, -1))
F32 = jnp.float32
BF16 = jnp.bfloat16
I32 = jnp.int32
MESH = pl.DeviceIdType.MESH


def iota(shape, dim):
    return lax.broadcasted_iota(I32, shape, dim)


def split(x):
    high = (x * 0.995).astype(BF16)
    low = (x - high.astype(F32)).astype(BF16)
    return high, low


def dot(a, b):
    return lax.dot_general(a, b, (((1,), (0,)), ((), ())), preferred_element_type=F32)


def dot_nt(a, b):
    return lax.dot_general(a, b, (((1,), (1,)), ((), ())), preferred_element_type=F32)


def roll(x, by, axis):
    return pltpu.roll(x, by % x.shape[axis], axis)


def onehot_rows(row, size):
    n = row.shape[1]
    return jnp.where(iota((size, n), 0) == row, 1.0, 0.0).astype(BF16)


def block_row(slot):
    block = slot >> 7
    return (block & 15) * CX + (block >> 4)


def flux_of(comps, coef, axis_n, move):
    nxt = [move(w, 1) for w in comps]

    def centred(w, w_next):
        return 7.0 / 12.0 * (w + w_next) - 1.0 / 12.0 * (move(w, -1) + move(w, 2))

    out = []
    for c in range(4):
        value = -0.5 * (nxt[c] - comps[c])
        if c == 0:
            value = value + centred(comps[1 + axis_n], nxt[1 + axis_n])
        if c == 1 + axis_n:
            value = value + centred(comps[0], nxt[0])
        out.append(coef * value)
    return out


def kernel(
    nx,
    ny,
    fields_hbm,
    pore_hbm,
    rate_hbm,
    part_hbm,
    occ_hbm,
    cell_hbm,
    send_hbm,
    count_hbm,
    land_hbm,
    fields_out,
    part_out,
    fields_ref,
    pore_ref,
    rate_ref,
    part_ref,
    occ_ref,
    cell_ref,
    send_ref,
    count_ref,
    land_ref,
    load_sem,
    state,
    split_state,
    values,
    deposit_hot,
    total,
    hx_out,
    hy_out,
    hx,
    hy,
    axial_out,
    axial_in,
    diag_out,
    diag_in,
    send_sem,
    recv_sem,
):
    ix = lax.axis_index("gx")
    iy = lax.axis_index("gy")

    def device(move):
        return (lax.rem(ix + move[0] + nx, nx), lax.rem(iy + move[1] + ny, ny))

    def present(move):
        x, y = ix - move[0], iy - move[1]
        return (x >= 0) & (x < nx) & (y >= 0) & (y < ny)

    loads = []
    for src, dst in (
        (rate_hbm, rate_ref),
        (cell_hbm, cell_ref),
        (part_hbm, part_ref),
        (occ_hbm, occ_ref),
        (send_hbm, send_ref),
        (count_hbm, count_ref),
        (pore_hbm, pore_ref),
        (fields_hbm, fields_ref),
        (land_hbm, land_ref),
    ):
        copy = pltpu.make_async_copy(src, dst, load_sem.at[len(loads)])
        copy.start()
        loads.append(copy)

    copies = []

    def send(src, dst, move):
        k = len(copies)
        copy = pltpu.make_async_remote_copy(
            src_ref=src,
            dst_ref=dst,
            send_sem=send_sem.at[k],
            recv_sem=recv_sem.at[k],
            device_id=device(move),
            device_id_type=MESH,
        )
        copy.start()
        copies.append(copy)
        return copy

    barrier = pltpu.get_barrier_semaphore()
    for move in MOVES:
        pl.semaphore_signal(barrier, inc=1, device_id=device(move), device_id_type=MESH)

    def lanes_of(y):
        return slice(y * SLOTS, (y + 1) * SLOTS)

    def rows_of(y):
        return slice(y * CX, (y + 1) * CX)

    loads[0].wait()
    loads[1].wait()
    rate = rate_ref[...]
    keep = jnp.exp(-rate)
    relax = jnp.exp(-rate / ROT)
    lane = iota((CX, SLOTS), 1)

    keep_slot, relax_slot = [], []
    for y in range(CY):
        half = slice((y // 8) * 128, (y // 8) * 128 + 128)
        index = cell_ref[:, lanes_of(y)] + (y % 8) * CZ
        keep_slot.append(jnp.take_along_axis(keep[:, half], index, axis=1))
        relax_slot.append(jnp.take_along_axis(relax[:, half], index, axis=1))

    for copy in loads[2:6]:
        copy.wait()
    occ = occ_ref[...]
    for y in range(CY):
        live = lane < occ[:, y : y + 1]
        for c in range(8):
            state[c, rows_of(y), :] = jnp.where(live, part_ref[c, :, lanes_of(y)], 0.0)

    def put_split(c, y, value):
        high, low = split(value)
        split_state[c * BLOCKS + y * CX : c * BLOCKS + (y + 1) * CX, 0:128] = high
        split_state[c * BLOCKS + y * CX : c * BLOCKS + (y + 1) * CX, 128:256] = low

    def send_list(step):
        slots, used = [], []
        for d in range(4):
            slots.append(send_ref[step * 8 + d])
            used.append(iota((1, CAP), 1) < count_ref[step * 8 + d])
        corner = diag_rows(send_ref, step)
        at = iota((1, 128), 1)
        ok = at < 0
        for d in range(4):
            ok = ok | ((at >= d * DIAG) & (at < d * DIAG + count_ref[step * 8 + 4 + d]))
        slots.append(corner)
        used.append(ok)
        return jnp.concatenate(slots, axis=1), [u.astype(I32) for u in used]

    def diag_rows(ref, step):
        at = iota((8, 128), 1) // DIAG
        out = jnp.zeros((8, 128), I32)
        for d in range(4):
            row = jnp.broadcast_to(ref[step * 8 + 4 + d][:, 0:128], (8, 128))
            out = jnp.where(at == d, roll(row, d * DIAG, 1), out)
        return out[0:1]

    def gather(step):
        slots, used = send_list(step)
        ok = jnp.concatenate(used, axis=1) > 0
        row = jnp.where(ok, block_row(slots), -1)
        place = slots & 127
        hot = []
        for start in range(0, LIST, 256):
            stop = min(start + 256, LIST)
            n = stop - start
            place_hot = onehot_rows(place[:, start:stop], SLOTS)
            hot.append(place_hot)
            mine = iota((BLOCKS, n), 0) == row[:, start:stop]
            product = dot(split_state[...], jnp.concatenate([place_hot, place_hot], axis=0))
            got = [
                jnp.sum(
                    jnp.where(mine, product[c * BLOCKS : (c + 1) * BLOCKS], 0.0),
                    axis=0,
                    keepdims=True,
                )
                for c in range(8)
            ]
            got = jnp.concatenate(got, axis=0)
            for tile in range(start // 128, stop // 128):
                piece = got[:, tile * 128 - start : tile * 128 - start + 128]
                if tile < AXIAL // 128:
                    at = (tile % 3) * 128
                    axial_out[step, tile // 3, :, at : at + 128] = piece
                else:
                    flag = jnp.broadcast_to(used[4].astype(F32), (8, 128))
                    diag_out[step] = jnp.where(
                        iota((8, 128), 1) < 64, piece, roll(flag, 64, 1)
                    )
        return row, jnp.concatenate(hot, axis=1)

    def send_particles(step):
        mine = []
        for d in range(4):
            mine.append(send(axial_out.at[step, d], axial_in.at[step, d], MOVES[d]))
        for d in range(4):
            mine.append(send(diag_out.at[step], diag_in.at[step, d], MOVES[4 + d]))
        return mine

    def deposit():
        for y in range(CY):
            w = state[6, rows_of(y), :]
            values[0, rows_of(y), :] = w
            for c in range(3):
                values[1 + c, rows_of(y), :] = w * state[3 + c, rows_of(y), :]
        own = iota((CY, FLAT), 1) // CZ == iota((CY, FLAT), 0)
        out = [[] for _ in range(4)]
        for x in range(CX):
            picked = jnp.concatenate(
                [values[c, pl.ds(x, CY, stride=CX), :] for c in range(4)], axis=0
            )
            high, low = split(picked)
            both = dot_nt(jnp.concatenate([high, low], axis=0), deposit_hot[x])
            both = both[: 4 * CY] + both[4 * CY :]
            for c in range(4):
                part = jnp.where(own, both[c * CY : (c + 1) * CY], 0.0)
                out[c].append(jnp.sum(part, axis=0, keepdims=True))
        return [jnp.concatenate(o, axis=0) for o in out]

    def pack_x(parts, shift):
        at = iota((8, FLAT), 0) // 2
        out = jnp.zeros((8, FLAT), F32)
        for i, part in enumerate(parts):
            out = jnp.where(at == i, roll(part, 2 * i - shift, 0), out)
        return out

    def pack_y(parts, shift):
        at = iota((CX, 128), 1) // 32
        out = jnp.zeros((CX, 128), F32)
        for i, part in enumerate(parts):
            out = jnp.where(at == i, roll(part, 32 * i - shift, 1), out)
        return out

    def send_halo(step):
        own = [total[step, c] for c in range(4)]
        hx_out[step, 0, 0] = pack_x([w[8:16] for w in own], 6)
        hx_out[step, 1, 0] = pack_x([w[0:8] for w in own], 0)
        hy_out[step, 0, 0] = pack_y([w[:, 128:256] for w in own], 96)
        hy_out[step, 1, 0] = pack_y([w[:, 0:128] for w in own], 0)
        if step == 0:
            for d in range(4):
                counts = [count_ref[s * 8 + d].astype(F32) for s in range(STEPS)]
                if d < 2:
                    rows = slice(8, 16) if d == 0 else slice(0, 8)
                    packed = pack_x([fluid[rows], keep[rows]], 6 if d == 0 else 0)
                    at = iota((8, FLAT), 0)
                    packed = jnp.where(at == 4, counts[0], jnp.where(at == 5, counts[1], packed))
                    hx_out[0, d, 1] = packed
                else:
                    lanes = slice(128, 256) if d == 2 else slice(0, 128)
                    packed = pack_y([fluid[:, lanes], keep[:, lanes]], 96 if d == 2 else 0)
                    at = iota((CX, 128), 1) // 32
                    packed = jnp.where(at == 2, counts[0], jnp.where(at == 3, counts[1], packed))
                    hy_out[0, d - 2, 1] = packed
            return [
                send(hx_out.at[0, 0], hx.at[0, 0], MOVES[0]),
                send(hx_out.at[0, 1], hx.at[0, 1], MOVES[1]),
                send(hy_out.at[0, 0], hy.at[0, 0], MOVES[2]),
                send(hy_out.at[0, 1], hy.at[0, 1], MOVES[3]),
            ]
        return [
            send(hx_out.at[step, 0, 0], hx.at[step, 0, 0], MOVES[0]),
            send(hx_out.at[step, 1, 0], hx.at[step, 1, 0], MOVES[1]),
            send(hy_out.at[step, 0, 0], hy.at[step, 0, 0], MOVES[2]),
            send(hy_out.at[step, 1, 0], hy.at[step, 1, 0], MOVES[3]),
        ]

    def ring_x(own, low, high, i):
        at = iota((8, FLAT), 0)
        low = jnp.where((at >= 6) & present(MOVES[0]), roll(low, 6 - 2 * i, 0), 0.0)
        edge = jnp.where((at < 2) & present(MOVES[1]), roll(high, -2 * i, 0), low)
        return jnp.concatenate([own, edge], axis=0)

    def ring_y(own, low, high, i):
        at = iota((CX, 128), 1)
        low = jnp.where((at >= 96) & present(MOVES[2]), roll(low, 96 - 32 * i, 1), 0.0)
        edge = jnp.where((at < 32) & present(MOVES[3]), roll(high, -32 * i, 1), low)
        return jnp.concatenate([own, edge], axis=1)

    def move_x(w, k):
        return roll(w, -k, 0)

    def move_y(w, k):
        return roll(w, -k * CZ, 1)

    zpos = iota((CX, FLAT), 1) % CZ

    def move_z(w, k):
        inside = (zpos + k >= 0) & (zpos + k < CZ)
        return jnp.where(inside, roll(w, -k, 1), 0.0)

    def coefs():
        def one(f, k, move):
            return f * move(f, 1) * (1.0 - 0.5 * (k + move(k, 1)))

        ex = [(hx[0, 0, 1], hx[0, 1, 1], i) for i in range(2)]
        ey = [(hy[0, 0, 1], hy[0, 1, 1], i) for i in range(2)]
        x = one(ring_x(fluid, *ex[0]), ring_x(keep, *ex[1]), move_x)
        y = one(ring_y(fluid, *ey[0]), ring_y(keep, *ey[1]), move_y)
        return x, y, one(fluid, keep, move_z)

    def divergence(step, coef):
        own = [total[step, c] for c in range(4)]
        xs = [ring_x(own[c], hx[step, 0, 0], hx[step, 1, 0], c) for c in range(4)]
        ys = [ring_y(own[c], hy[step, 0, 0], hy[step, 1, 0], c) for c in range(4)]
        fx = flux_of(xs, coef[0], 0, move_x)
        fy = flux_of(ys, coef[1], 1, move_y)
        fz = flux_of(own, coef[2], 2, move_z)
        out = []
        for c in range(4):
            dx = (fx[c] - move_x(fx[c], -1))[:CX]
            dy = (fy[c] - move_y(fy[c], -1))[:, :FLAT]
            out.append(dx + dy + (fz[c] - move_z(fz[c], -1)))
        return out

    def collide(c, y, value):
        rows = rows_of(y)
        if c < 3:
            return value + COURANT * state[3 + c, rows, :]
        if c == 6:
            return value * keep_slot[y]
        return 1.0 + (value - 1.0) * relax_slot[y]

    def land_list(step):
        rows, places, parts = [], [], []
        at = iota((1, CAP), 1)
        for d in range(4):
            got = axial_in[step, d]
            if d < 2:
                count = hx[0, d, 1][4 + step : 5 + step, 0:1]
            else:
                count = hy[0, d - 2, 1][0:1, 64 + 32 * step : 65 + 32 * step]
            fit = at.astype(F32) < jnp.broadcast_to(count, (1, CAP))
            fit = fit & present(MOVES[d])
            slot = land_ref[step * 8 + d]
            rows.append(jnp.where(fit, block_row(slot), -1))
            places.append(slot & 127)
            parts.append(jnp.where(jnp.broadcast_to(fit.astype(F32), (8, CAP)) > 0, got, 0.0))
        at = iota((8, 128), 1)
        got = jnp.zeros((8, 128), F32)
        for d in range(4):
            mine = (at % 64) // DIAG == d
            got = jnp.where(mine & present(MOVES[4 + d]), diag_in[step, d], got)
        fit = (roll(got, 64, 1) > 0.5) & (at < 64)
        slot = diag_rows(land_ref, step)
        rows.append(jnp.where(fit, block_row(jnp.broadcast_to(slot, (8, 128))), -1)[0:1])
        places.append(slot & 127)
        parts.append(jnp.where(fit, got, 0.0))
        return (
            jnp.concatenate(parts, axis=1),
            jnp.concatenate(rows, axis=1),
            jnp.concatenate(places, axis=1),
        )

    def land(comps, arrived, row_hot, place_hot):
        out = []
        for first in range(0, len(comps), 2):
            highs, lows = [], []
            for c in comps[first : first + 2]:
                high, low = split(arrived[c : c + 1])
                highs.append(place_hot * high)
                lows.append(place_hot * low)
            got = dot_nt(row_hot, jnp.concatenate(highs, axis=0)) + dot_nt(
                row_hot, jnp.concatenate(lows, axis=0)
            )
            out += [got[:, :128], got[:, 128:]]
        return out

    for y in range(CY):
        for c in (0, 1, 2, 6, 7):
            put_split(c, y, collide(c, y, state[c, rows_of(y), :]))
        for c in (3, 4, 5):
            put_split(c, y, state[c, rows_of(y), :])
    sent = [gather(0)]

    pl.semaphore_wait(barrier, len(MOVES))
    arrivals = [send_particles(0)]

    for x in range(CX):
        for y in range(CY):
            mine = iota((CZ, SLOTS), 0) == jnp.broadcast_to(
                cell_ref[x : x + 1, lanes_of(y)], (CZ, SLOTS)
            )
            deposit_hot[x, y * CZ : (y + 1) * CZ, :] = jnp.where(mine, 1.0, 0.0).astype(BF16)
    moments = deposit()
    for copy in loads[6:]:
        copy.wait()
    fluid = pore_ref[...].astype(F32)
    for c in range(4):
        total[0, c] = (fields_ref[c] + moments[c]) * fluid
    halos = [send_halo(0)]

    for y in range(CY):
        for c in (0, 1, 2, 6, 7):
            value = collide(c, y, state[c, rows_of(y), :])
            state[c, rows_of(y), :] = value
            put_split(c, y, collide(c, y, value))
    sent.append(gather(1))
    arrivals.append(send_particles(1))

    for copy in halos[0]:
        copy.wait()
    coef = coefs()
    div = divergence(0, coef)
    fields = [
        fields_ref[c] - COURANT * div[c] + (1.0 - keep) * moments[c] for c in range(4)
    ]

    everything = tuple(range(8))
    for step in range(STEPS):
        for copy in arrivals[step]:
            copy.wait()
        arrived, row, place = land_list(step)
        row_hot = onehot_rows(row, BLOCKS)
        place_hot = onehot_rows(place, SLOTS)
        sent_row, sent_place = sent[step]
        cleared = (dot_nt(row_hot, place_hot) + dot_nt(onehot_rows(sent_row, BLOCKS), sent_place)) > 0.5

        def settle(comps):
            news = land(comps, arrived, row_hot, place_hot)
            for c, new in zip(comps, news):
                state[c] = jnp.where(cleared, 0.0, state[c]) + new

        if step == 0:
            settle((6, 3, 4, 5))
            moments = deposit()
            for c in range(4):
                total[1, c] = (fields[c] + moments[c]) * fluid
            halos.append(send_halo(1))
            settle((0, 1, 2, 7))
            for y in range(CY):
                for c in (0, 1, 2, 6, 7):
                    state[c, rows_of(y), :] = collide(c, y, state[c, rows_of(y), :])
        else:
            settle(everything)

    for y in range(CY):
        for c in range(8):
            part_out[c, :, lanes_of(y)] = state[c, rows_of(y), :]
    for copy in halos[1]:
        copy.wait()
    div = divergence(1, coef)
    for c in range(4):
        fields_out[c] = fields[c] - COURANT * div[c] + (1.0 - keep) * moments[c]


def solution(mesh):
    nx, ny = mesh.shape["gx"], mesh.shape["gy"]

    def body(fields, pore, rate, particles, occupancy, slot_cell, send_slot, send_count, land_slot):
        vmem = pl.BlockSpec(memory_space=pltpu.VMEM)
        hbm = pl.BlockSpec(memory_space=pltpu.HBM)
        copies = 8 * STEPS + 4 * STEPS

        def run(*refs):
            kernel(nx, ny, *refs)

        return pl.pallas_call(
            run,
            out_shape=(
                jax.ShapeDtypeStruct(fields.shape, F32),
                jax.ShapeDtypeStruct(particles.shape, F32),
            ),
            in_specs=[hbm] * 9,
            out_specs=(vmem, vmem),
            scratch_shapes=[
                pltpu.VMEM(fields.shape, F32),
                pltpu.VMEM(pore.shape, I32),
                pltpu.VMEM(rate.shape, F32),
                pltpu.VMEM(particles.shape, F32),
                pltpu.VMEM(occupancy.shape, I32),
                pltpu.VMEM(slot_cell.shape, I32),
                pltpu.VMEM(send_slot.shape, I32),
                pltpu.SMEM((STEPS * 8,), I32),
                pltpu.VMEM(land_slot.shape, I32),
                pltpu.SemaphoreType.DMA((9,)),
                pltpu.VMEM((8, BLOCKS, SLOTS), F32),
                pltpu.VMEM((8 * BLOCKS, 2 * SLOTS), BF16),
                pltpu.VMEM((4, BLOCKS, SLOTS), F32),
                pltpu.VMEM((CX, FLAT, SLOTS), BF16),
                pltpu.VMEM((STEPS, 4, CX, FLAT), F32),
                pltpu.VMEM((STEPS, 2, 2, 8, FLAT), F32),
                pltpu.VMEM((STEPS, 2, 2, CX, 128), F32),
                pltpu.VMEM((STEPS, 2, 2, 8, FLAT), F32),
                pltpu.VMEM((STEPS, 2, 2, CX, 128), F32),
                pltpu.VMEM((STEPS, 4, 8, CAP), F32),
                pltpu.VMEM((STEPS, 4, 8, CAP), F32),
                pltpu.VMEM((STEPS, 8, 128), F32),
                pltpu.VMEM((STEPS, 4, 8, 128), F32),
                pltpu.SemaphoreType.DMA((copies,)),
                pltpu.SemaphoreType.DMA((copies,)),
            ],
            compiler_params=pltpu.CompilerParams(
                collective_id=0, has_side_effects=True, vmem_limit_bytes=48 << 20
            ),
        )(
            *[
                pltpu.with_memory_space_constraint(x, pltpu.HBM)
                for x in (
                    fields,
                    pore,
                    rate,
                    particles,
                    occupancy,
                    slot_cell,
                    send_slot,
                    send_count.reshape(STEPS * 8),
                    land_slot,
                )
            ]
        )

    return jax.shard_map(
        body,
        mesh=mesh,
        in_specs=(
            P(None, "gx", "gy"),
            P("gx", "gy"),
            P("gx", "gy"),
            P(None, "gx", "gy"),
            P("gx", "gy"),
            P("gx", "gy"),
            P(None, "gx", "gy"),
            P(None, "gx", "gy"),
            P(None, "gx", "gy"),
        ),
        out_specs=(P(None, "gx", "gy"), P(None, "gx", "gy")),
        check_vma=False,
    )
```

```python
import jax
import jax.numpy as jnp
from jax import lax
from jax.experimental import pallas as pl
from jax.experimental.pallas import tpu as pltpu
from jax.sharding import PartitionSpec as P

CX = 16
CY = 16
CZ = 16
SLOTS = 128
STEPS = 2
CAP = 384
DIAG = 16
BLOCKS = CX * CY
FLAT = CY * CZ
AXIAL = 4 * CAP
LIST = AXIAL + 128
COURANT = 0.25
ROT = 4.0
MOVES = ((1, 0), (-1, 0), (0, 1), (0, -1), (1, 1), (1, -1), (-1, 1), (-1, -1))
F32 = jnp.float32
BF16 = jnp.bfloat16
I32 = jnp.int32
MESH = pl.DeviceIdType.MESH


def iota(shape, dim):
    return lax.broadcasted_iota(I32, shape, dim)


def split(x):
    high = (x * 0.995).astype(BF16)
    low = (x - high.astype(F32)).astype(BF16)
    return high, low


def dot(a, b):
    return lax.dot_general(a, b, (((1,), (0,)), ((), ())), preferred_element_type=F32)


def dot_nt(a, b):
    return lax.dot_general(a, b, (((1,), (1,)), ((), ())), preferred_element_type=F32)


def roll(x, by, axis):
    return pltpu.roll(x, by % x.shape[axis], axis)


def onehot_rows(row, size):
    n = row.shape[1]
    return jnp.where(iota((size, n), 0) == row, 1.0, 0.0).astype(BF16)


def block_row(slot):
    block = slot >> 7
    return (block & 15) * CX + (block >> 4)


def flux_of(comps, coef, axis_n, move):
    nxt = [move(w, 1) for w in comps]

    def centred(w, w_next):
        return 7.0 / 12.0 * (w + w_next) - 1.0 / 12.0 * (move(w, -1) + move(w, 2))

    out = []
    for c in range(4):
        value = -0.5 * (nxt[c] - comps[c])
        if c == 0:
            value = value + centred(comps[1 + axis_n], nxt[1 + axis_n])
        if c == 1 + axis_n:
            value = value + centred(comps[0], nxt[0])
        out.append(coef * value)
    return out


def kernel(
    nx,
    ny,
    fields_hbm,
    pore_hbm,
    rate_hbm,
    part_hbm,
    occ_hbm,
    cell_hbm,
    send_hbm,
    count_hbm,
    land_hbm,
    fields_out,
    part_out,
    fields_ref,
    pore_ref,
    rate_ref,
    part_ref,
    occ_ref,
    cell_ref,
    send_ref,
    count_ref,
    land_ref,
    load_sem,
    state,
    weight_one,
    split_state,
    values,
    deposit_hot,
    total,
    hx_out,
    hy_out,
    hx,
    hy,
    axial_out,
    axial_in,
    diag_out,
    diag_in,
    send_sem,
    recv_sem,
):
    ix = lax.axis_index("gx")
    iy = lax.axis_index("gy")

    def device(move):
        return (lax.rem(ix + move[0] + nx, nx), lax.rem(iy + move[1] + ny, ny))

    def present(move):
        x, y = ix - move[0], iy - move[1]
        return (x >= 0) & (x < nx) & (y >= 0) & (y < ny)

    loads = []
    for src, dst in (
        (rate_hbm, rate_ref),
        (cell_hbm, cell_ref),
        (part_hbm, part_ref),
        (occ_hbm, occ_ref),
        (send_hbm, send_ref),
        (count_hbm, count_ref),
        (pore_hbm, pore_ref),
        (fields_hbm, fields_ref),
        (land_hbm, land_ref),
    ):
        copy = pltpu.make_async_copy(src, dst, load_sem.at[len(loads)])
        copy.start()
        loads.append(copy)

    copies = []

    def send(src, dst, move):
        k = len(copies)
        copy = pltpu.make_async_remote_copy(
            src_ref=src,
            dst_ref=dst,
            send_sem=send_sem.at[k],
            recv_sem=recv_sem.at[k],
            device_id=device(move),
            device_id_type=MESH,
        )
        copy.start()
        copies.append(copy)
        return copy

    barrier = pltpu.get_barrier_semaphore()
    for move in MOVES:
        pl.semaphore_signal(barrier, inc=1, device_id=device(move), device_id_type=MESH)

    def lanes_of(y):
        return slice(y * SLOTS, (y + 1) * SLOTS)

    def rows_of(y):
        return slice(y * CX, (y + 1) * CX)

    loads[0].wait()
    loads[1].wait()
    rate = rate_ref[...]
    keep = jnp.exp(-rate)
    relax = jnp.exp(-rate / ROT)
    lane = iota((CX, SLOTS), 1)

    keep_slot, relax_slot = [], []
    for y in range(CY):
        half = slice((y // 8) * 128, (y // 8) * 128 + 128)
        index = cell_ref[:, lanes_of(y)] + (y % 8) * CZ
        keep_slot.append(jnp.take_along_axis(keep[:, half], index, axis=1))
        relax_slot.append(jnp.take_along_axis(relax[:, half], index, axis=1))

    for copy in loads[2:6]:
        copy.wait()
    occ = occ_ref[...]
    for y in range(CY):
        live = lane < occ[:, y : y + 1]
        for c in range(8):
            state[c, rows_of(y), :] = jnp.where(live, part_ref[c, :, lanes_of(y)], 0.0)

    def put_split(k, y, value):
        high, low = split(value)
        rows = slice(k * BLOCKS + y * CX, k * BLOCKS + (y + 1) * CX)
        split_state[rows, 0:128] = high
        split_state[rows, 128:256] = low

    def diag_rows(ref, step):
        at = iota((8, 128), 1) // DIAG
        out = jnp.zeros((8, 128), I32)
        for d in range(4):
            row = jnp.broadcast_to(ref[step * 8 + 4 + d][:, 0:128], (8, 128))
            out = jnp.where(at == d, roll(row, d * DIAG, 1), out)
        return out[0:1]

    def slots_of(ref, step):
        slots = [ref[step * 8 + d] for d in range(4)] + [diag_rows(ref, step)]
        return jnp.concatenate(slots, axis=1)

    def send_list(step):
        slots = slots_of(send_ref, step)
        used = [
            (iota((1, CAP), 1) < count_ref[step * 8 + d]).astype(I32) for d in range(4)
        ]
        at = iota((1, 128), 1)
        ok = at < 0
        for d in range(4):
            ok = ok | ((at >= d * DIAG) & (at < d * DIAG + count_ref[step * 8 + 4 + d]))
        used.append(ok.astype(I32))
        row = jnp.where(jnp.concatenate(used, axis=1) > 0, block_row(slots), -1)
        flag = roll(jnp.broadcast_to(used[4].astype(F32), (4, 128)), 64, 1)
        return row, onehot_rows(slots & 127, SLOTS), flag

    def gather(listed, first, parts):
        row, place_hot, flag = listed
        count = 4 * len(parts)
        for start in range(0, LIST, 256):
            stop = min(start + 256, LIST)
            n = stop - start
            hot = place_hot[:, start:stop]
            mine = iota((BLOCKS, n), 0) == row[:, start:stop]
            product = dot(
                split_state[first * BLOCKS : (first + count) * BLOCKS, :],
                jnp.concatenate([hot, hot], axis=0),
            )
            got = [
                jnp.sum(
                    jnp.where(mine, product[c * BLOCKS : (c + 1) * BLOCKS], 0.0),
                    axis=0,
                    keepdims=True,
                )
                for c in range(count)
            ]
            for i, part in enumerate(parts):
                four = jnp.concatenate(got[4 * i : 4 * i + 4], axis=0)
                for tile in range(start // 128, stop // 128):
                    piece = four[:, tile * 128 - start : tile * 128 - start + 128]
                    if tile < AXIAL // 128:
                        at = (tile % 3) * 128
                        axial_out[tile // 3, part, :, at : at + 128] = piece
                    else:
                        diag_out[part] = jnp.where(iota((4, 128), 1) < 64, piece, flag)

    def send_particles(first, count):
        mine = []
        parts = pl.ds(first, count)
        for d in range(4):
            mine.append(send(axial_out.at[d, parts], axial_in.at[d, parts], MOVES[d]))
        for d in range(4):
            mine.append(send(diag_out.at[parts], diag_in.at[d, parts], MOVES[4 + d]))
        return mine

    def deposit(weight):
        for y in range(CY):
            w = weight(y)
            values[0, rows_of(y), :] = w
            for c in range(3):
                values[1 + c, rows_of(y), :] = w * state[3 + c, rows_of(y), :]
        own = iota((CY, FLAT), 1) // CZ == iota((CY, FLAT), 0)
        out = [[] for _ in range(4)]
        for x in range(CX):
            picked = jnp.concatenate(
                [values[c, pl.ds(x, CY, stride=CX), :] for c in range(4)], axis=0
            )
            high, low = split(picked)
            both = dot_nt(jnp.concatenate([high, low], axis=0), deposit_hot[x])
            both = both[: 4 * CY] + both[4 * CY :]
            for c in range(4):
                part = jnp.where(own, both[c * CY : (c + 1) * CY], 0.0)
                out[c].append(jnp.sum(part, axis=0, keepdims=True))
        return [jnp.concatenate(o, axis=0) for o in out]

    def pack_x(parts, shift):
        at = iota((8, FLAT), 0) // 2
        out = jnp.zeros((8, FLAT), F32)
        for i, part in enumerate(parts):
            out = jnp.where(at == i, roll(part, 2 * i - shift, 0), out)
        return out

    def pack_y(parts, shift):
        at = iota((CX, 128), 1) // 32
        out = jnp.zeros((CX, 128), F32)
        for i, part in enumerate(parts):
            out = jnp.where(at == i, roll(part, 32 * i - shift, 1), out)
        return out

    def send_halo(step):
        own = [total[step, c] for c in range(4)]
        hx_out[step, 0, 0] = pack_x([w[8:16] for w in own], 6)
        hx_out[step, 1, 0] = pack_x([w[0:8] for w in own], 0)
        hy_out[step, 0, 0] = pack_y([w[:, 128:256] for w in own], 96)
        hy_out[step, 1, 0] = pack_y([w[:, 0:128] for w in own], 0)
        if step == 0:
            for d in range(4):
                counts = [count_ref[s * 8 + d].astype(F32) for s in range(STEPS)]
                if d < 2:
                    rows = slice(8, 16) if d == 0 else slice(0, 8)
                    packed = pack_x([fluid[rows], keep[rows]], 6 if d == 0 else 0)
                    at = iota((8, FLAT), 0)
                    packed = jnp.where(at == 4, counts[0], jnp.where(at == 5, counts[1], packed))
                    hx_out[0, d, 1] = packed
                else:
                    lanes = slice(128, 256) if d == 2 else slice(0, 128)
                    packed = pack_y([fluid[:, lanes], keep[:, lanes]], 96 if d == 2 else 0)
                    at = iota((CX, 128), 1) // 32
                    packed = jnp.where(at == 2, counts[0], jnp.where(at == 3, counts[1], packed))
                    hy_out[0, d - 2, 1] = packed
            return [
                send(hx_out.at[0, 0], hx.at[0, 0], MOVES[0]),
                send(hx_out.at[0, 1], hx.at[0, 1], MOVES[1]),
                send(hy_out.at[0, 0], hy.at[0, 0], MOVES[2]),
                send(hy_out.at[0, 1], hy.at[0, 1], MOVES[3]),
            ]
        return [
            send(hx_out.at[step, 0, 0], hx.at[step, 0, 0], MOVES[0]),
            send(hx_out.at[step, 1, 0], hx.at[step, 1, 0], MOVES[1]),
            send(hy_out.at[step, 0, 0], hy.at[step, 0, 0], MOVES[2]),
            send(hy_out.at[step, 1, 0], hy.at[step, 1, 0], MOVES[3]),
        ]

    def ring_x(own, low, high, i):
        at = iota((8, FLAT), 0)
        low = jnp.where((at >= 6) & present(MOVES[0]), roll(low, 6 - 2 * i, 0), 0.0)
        edge = jnp.where((at < 2) & present(MOVES[1]), roll(high, -2 * i, 0), low)
        return jnp.concatenate([own, edge], axis=0)

    def ring_y(own, low, high, i):
        at = iota((CX, 128), 1)
        low = jnp.where((at >= 96) & present(MOVES[2]), roll(low, 96 - 32 * i, 1), 0.0)
        edge = jnp.where((at < 32) & present(MOVES[3]), roll(high, -32 * i, 1), low)
        return jnp.concatenate([own, edge], axis=1)

    def move_x(w, k):
        return roll(w, -k, 0)

    def move_y(w, k):
        return roll(w, -k * CZ, 1)

    zpos = iota((CX, FLAT), 1) % CZ

    def move_z(w, k):
        inside = (zpos + k >= 0) & (zpos + k < CZ)
        return jnp.where(inside, roll(w, -k, 1), 0.0)

    def coefs():
        def one(f, k, move):
            return f * move(f, 1) * (1.0 - 0.5 * (k + move(k, 1)))

        ex = [(hx[0, 0, 1], hx[0, 1, 1], i) for i in range(2)]
        ey = [(hy[0, 0, 1], hy[0, 1, 1], i) for i in range(2)]
        x = one(ring_x(fluid, *ex[0]), ring_x(keep, *ex[1]), move_x)
        y = one(ring_y(fluid, *ey[0]), ring_y(keep, *ey[1]), move_y)
        return x, y, one(fluid, keep, move_z)

    def divergence(step, coef):
        own = [total[step, c] for c in range(4)]
        xs = [ring_x(own[c], hx[step, 0, 0], hx[step, 1, 0], c) for c in range(4)]
        ys = [ring_y(own[c], hy[step, 0, 0], hy[step, 1, 0], c) for c in range(4)]
        fx = flux_of(xs, coef[0], 0, move_x)
        fy = flux_of(ys, coef[1], 1, move_y)
        fz = flux_of(own, coef[2], 2, move_z)
        out = []
        for c in range(4):
            dx = (fx[c] - move_x(fx[c], -1))[:CX]
            dy = (fy[c] - move_y(fy[c], -1))[:, :FLAT]
            out.append(dx + dy + (fz[c] - move_z(fz[c], -1)))
        return out

    def collide(c, y, value):
        rows = rows_of(y)
        if c < 3:
            return value + COURANT * state[3 + c, rows, :]
        if c == 6:
            return value * keep_slot[y]
        return 1.0 + (value - 1.0) * relax_slot[y]

    def arrived(step, rows):
        at = iota((1, CAP), 1).astype(F32)
        fits = []
        for d in range(4):
            if d < 2:
                count = hx[0, d, 1][4 + step : 5 + step, 0:1]
            else:
                count = hy[0, d - 2, 1][0:1, 64 + 32 * step : 65 + 32 * step]
            fits.append((at < jnp.broadcast_to(count, (1, CAP))) & present(MOVES[d]))
        lane = iota((4, 128), 1)
        corners = {}
        for part in sorted({part for part, _ in rows}):
            got = jnp.zeros((4, 128), F32)
            for d in range(4):
                mine = (lane % 64) // DIAG == d
                got = jnp.where(mine & present(MOVES[4 + d]), diag_in[d, part], got)
            corners[part] = got
        got = corners[rows[0][0]]
        flag = (roll(got, 64, 1) > 0.5) & (lane < 64)
        fits.append(flag[0:1])
        fit = jnp.concatenate([f.astype(F32) for f in fits], axis=1) > 0.5
        out = []
        for part, at in rows:
            pieces = [axial_in[d, part, at : at + 1, :] for d in range(4)]
            pieces.append(corners[part][at : at + 1])
            out.append(jnp.where(fit, jnp.concatenate(pieces, axis=1), 0.0))
        return out, fit

    for y in range(CY):
        w = collide(6, y, state[6, rows_of(y), :])
        weight_one[rows_of(y), :] = w
        put_split(0, y, w)
        for c in range(3):
            put_split(1 + c, y, state[3 + c, rows_of(y), :])
    listed = [send_list(0)]
    gather(listed[0], 0, [0])
    pl.semaphore_wait(barrier, len(MOVES))
    first = send_particles(0, 1)

    for x in range(CX):
        for y in range(CY):
            mine = iota((CZ, SLOTS), 0) == jnp.broadcast_to(
                cell_ref[x : x + 1, lanes_of(y)], (CZ, SLOTS)
            )
            deposit_hot[x, y * CZ : (y + 1) * CZ, :] = jnp.where(mine, 1.0, 0.0).astype(BF16)
    moments = deposit(lambda y: state[6, rows_of(y), :])
    for copy in loads[6:]:
        copy.wait()
    fluid = pore_ref[...].astype(F32)
    for c in range(4):
        total[0, c] = (fields_ref[c] + moments[c]) * fluid
    halo = send_halo(0)

    for y in range(CY):
        for k, c in enumerate((0, 1, 2, 7)):
            value = collide(c, y, state[c, rows_of(y), :])
            put_split(9 + k, y, value)
            value = collide(c, y, value)
            put_split(5 + k, y, value)
            state[c, rows_of(y), :] = value
        value = collide(6, y, weight_one[rows_of(y), :])
        put_split(4, y, value)
        state[6, rows_of(y), :] = value
    listed.append(send_list(1))
    gather(listed[0], 9, [1])
    gather(listed[1], 1, [2, 3])
    late = send_particles(1, 3)

    sent_hot = onehot_rows(listed[0][0], BLOCKS)
    sent = dot_nt(sent_hot, listed[0][1])
    stay = deposit(lambda y: jnp.where(sent[rows_of(y)] > 0.5, 0.0, weight_one[rows_of(y), :]))

    slots = [slots_of(land_ref, step) for step in range(STEPS)]
    places = [onehot_rows(t & 127, SLOTS) for t in slots]
    row = block_row(slots[0])
    cell_all = jnp.concatenate([cell_ref[:, lanes_of(y)] for y in range(CY)], axis=0)
    found = dot(cell_all.astype(F32).astype(BF16), places[0])
    z = jnp.sum(
        jnp.where(iota((BLOCKS, LIST), 0) == row, found, 0.0), axis=0, keepdims=True
    )
    flat_cell = (row >> 4).astype(F32) * CZ + z
    cell_hot = jnp.where(
        iota((FLAT, LIST), 0).astype(F32) == flat_cell, 1.0, 0.0
    ).astype(BF16)
    x_mine = iota((CX, LIST), 0) == (row & 15)
    table = jnp.concatenate([*split(keep), *split(relax)], axis=0)
    factors = dot(table, cell_hot)

    def factor(k):
        both = factors[2 * k * CX : (2 * k + 1) * CX] + factors[(2 * k + 1) * CX : (2 * k + 2) * CX]
        return jnp.sum(jnp.where(x_mine, both, 0.0), axis=0, keepdims=True)

    keep_land, relax_land = factor(0), factor(1)

    for copy in first + halo:
        copy.wait()
    (w, vx, vy, vz), fit = arrived(0, [(0, k) for k in range(4)])
    highs, lows = [], []
    for value in (w, w * vx, w * vy, w * vz):
        high, low = split(jnp.where(x_mine, value, 0.0))
        highs.append(high)
        lows.append(low)
    landed = dot_nt(jnp.concatenate(highs + lows, axis=0), cell_hot)
    landed = landed[: 4 * CX] + landed[4 * CX :]
    coef = coefs()
    div = divergence(0, coef)
    fields = [
        fields_ref[c] - COURANT * div[c] + (1.0 - keep) * moments[c] for c in range(4)
    ]
    moments = [stay[c] + landed[c * CX : (c + 1) * CX] for c in range(4)]
    for c in range(4):
        total[1, c] = (fields[c] + moments[c]) * fluid
    halo = send_halo(1)

    for copy in late:
        copy.wait()
    (px, py, pz, rot), _ = arrived(0, [(1, k) for k in range(4)])
    two, fit_two = arrived(1, [(3, 0), (3, 1), (3, 2), (2, 0), (2, 1), (2, 2), (2, 3), (3, 3)])
    one = [
        px + COURANT * vx,
        py + COURANT * vy,
        pz + COURANT * vz,
        vx,
        vy,
        vz,
        w * keep_land,
        jnp.where(fit, 1.0 + (rot - 1.0) * relax_land, 0.0),
    ]
    arrivals = [jnp.concatenate([a, b], axis=1) for a, b in zip(one, two)]
    rows = jnp.concatenate(
        [jnp.where(f, block_row(t), -1) for f, t in zip((fit, fit_two), slots)], axis=1
    )
    row_hot = onehot_rows(rows, BLOCKS)
    place_hot = jnp.concatenate(places, axis=1)
    for y in range(CY):
        rot = jnp.where(sent[rows_of(y)] > 0.5, 1.0 - relax_slot[y], state[7, rows_of(y), :])
        state[7, rows_of(y), :] = rot
    new = dot_nt(onehot_rows(listed[1][0], BLOCKS), listed[1][1]) + dot_nt(row_hot, place_hot)
    cleared = [sent + new > 0.5] * 7 + [new > 0.5]
    for c in range(0, 8, 2):
        highs, lows = [], []
        for k in (c, c + 1):
            high, low = split(arrivals[k])
            highs.append(place_hot * high)
            lows.append(place_hot * low)
        got = dot_nt(row_hot, jnp.concatenate(highs, axis=0)) + dot_nt(
            row_hot, jnp.concatenate(lows, axis=0)
        )
        for k in (0, 1):
            new = jnp.where(cleared[c + k], 0.0, state[c + k]) + got[:, k * 128 : (k + 1) * 128]
            for y in range(CY):
                part_out[c + k, :, lanes_of(y)] = new[rows_of(y)]
    for copy in halo:
        copy.wait()
    div = divergence(1, coef)
    for c in range(4):
        fields_out[c] = fields[c] - COURANT * div[c] + (1.0 - keep) * moments[c]


def solution(mesh):
    nx, ny = mesh.shape["gx"], mesh.shape["gy"]

    def body(fields, pore, rate, particles, occupancy, slot_cell, send_slot, send_count, land_slot):
        vmem = pl.BlockSpec(memory_space=pltpu.VMEM)
        hbm = pl.BlockSpec(memory_space=pltpu.HBM)
        copies = 8 * STEPS + 4 * STEPS

        def run(*refs):
            kernel(nx, ny, *refs)

        return pl.pallas_call(
            run,
            out_shape=(
                jax.ShapeDtypeStruct(fields.shape, F32),
                jax.ShapeDtypeStruct(particles.shape, F32),
            ),
            in_specs=[hbm] * 9,
            out_specs=(vmem, vmem),
            scratch_shapes=[
                pltpu.VMEM(fields.shape, F32),
                pltpu.VMEM(pore.shape, I32),
                pltpu.VMEM(rate.shape, F32),
                pltpu.VMEM(particles.shape, F32),
                pltpu.VMEM(occupancy.shape, I32),
                pltpu.VMEM(slot_cell.shape, I32),
                pltpu.VMEM(send_slot.shape, I32),
                pltpu.SMEM((STEPS * 8,), I32),
                pltpu.VMEM(land_slot.shape, I32),
                pltpu.SemaphoreType.DMA((9,)),
                pltpu.VMEM((8, BLOCKS, SLOTS), F32),
                pltpu.VMEM((BLOCKS, SLOTS), F32),
                pltpu.VMEM((13 * BLOCKS, 2 * SLOTS), BF16),
                pltpu.VMEM((4, BLOCKS, SLOTS), F32),
                pltpu.VMEM((CX, FLAT, SLOTS), BF16),
                pltpu.VMEM((STEPS, 4, CX, FLAT), F32),
                pltpu.VMEM((STEPS, 2, 2, 8, FLAT), F32),
                pltpu.VMEM((STEPS, 2, 2, CX, 128), F32),
                pltpu.VMEM((STEPS, 2, 2, 8, FLAT), F32),
                pltpu.VMEM((STEPS, 2, 2, CX, 128), F32),
                pltpu.VMEM((4, 4, 4, CAP), F32),
                pltpu.VMEM((4, 4, 4, CAP), F32),
                pltpu.VMEM((4, 4, 128), F32),
                pltpu.VMEM((4, 4, 4, 128), F32),
                pltpu.SemaphoreType.DMA((copies,)),
                pltpu.SemaphoreType.DMA((copies,)),
            ],
            compiler_params=pltpu.CompilerParams(
                collective_id=0, has_side_effects=True, vmem_limit_bytes=48 << 20
            ),
        )(
            *[
                pltpu.with_memory_space_constraint(x, pltpu.HBM)
                for x in (
                    fields,
                    pore,
                    rate,
                    particles,
                    occupancy,
                    slot_cell,
                    send_slot,
                    send_count.reshape(STEPS * 8),
                    land_slot,
                )
            ]
        )

    return jax.shard_map(
        body,
        mesh=mesh,
        in_specs=(
            P(None, "gx", "gy"),
            P("gx", "gy"),
            P("gx", "gy"),
            P(None, "gx", "gy"),
            P("gx", "gy"),
            P("gx", "gy"),
            P(None, "gx", "gy"),
            P(None, "gx", "gy"),
            P(None, "gx", "gy"),
        ),
        out_specs=(P(None, "gx", "gy"), P(None, "gx", "gy")),
        check_vma=False,
    )
```

```python
import jax
import jax.numpy as jnp
from jax import lax
from jax.experimental import pallas as pl
from jax.experimental.pallas import tpu as pltpu
from jax.sharding import PartitionSpec as P

CX = 16
CY = 16
CZ = 16
SLOTS = 128
STEPS = 2
CAP = 384
DIAG = 16
BLOCKS = CX * CY
FLAT = CY * CZ
AXIAL = 4 * CAP
LIST = AXIAL + 128
LIVE = 96
DEAD = 32
SPAN = SLOTS - DEAD
COURANT = 0.25
ROT = 4.0
MOVES = ((1, 0), (-1, 0), (0, 1), (0, -1), (1, 1), (1, -1), (-1, 1), (-1, -1))
F32 = jnp.float32
BF16 = jnp.bfloat16
I32 = jnp.int32
MESH = pl.DeviceIdType.MESH


def iota(shape, dim):
    return lax.broadcasted_iota(I32, shape, dim)


def split(x):
    high = (x * 0.995).astype(BF16)
    low = (x - high.astype(F32)).astype(BF16)
    return high, low


def dot(a, b):
    return lax.dot_general(a, b, (((1,), (0,)), ((), ())), preferred_element_type=F32)


def dot_nt(a, b):
    return lax.dot_general(a, b, (((1,), (1,)), ((), ())), preferred_element_type=F32)


def roll(x, by, axis):
    return pltpu.roll(x, by % x.shape[axis], axis)


def onehot_rows(row, size):
    n = row.shape[1]
    return jnp.where(iota((size, n), 0) == row, 1.0, 0.0).astype(BF16)


def block_row(slot):
    block = slot >> 7
    return (block & 15) * CX + (block >> 4)


def flux_of(comps, coef, axis_n, move):
    nxt = [move(w, 1) for w in comps]

    def centred(w, w_next):
        return 7.0 / 12.0 * (w + w_next) - 1.0 / 12.0 * (move(w, -1) + move(w, 2))

    out = []
    for c in range(4):
        value = -0.5 * (nxt[c] - comps[c])
        if c == 0:
            value = value + centred(comps[1 + axis_n], nxt[1 + axis_n])
        if c == 1 + axis_n:
            value = value + centred(comps[0], nxt[0])
        out.append(coef * value)
    return out


def kernel(
    nx,
    ny,
    fields_hbm,
    pore_hbm,
    rate_hbm,
    part_hbm,
    occ_hbm,
    cell_hbm,
    send_hbm,
    count_hbm,
    land_hbm,
    fields_out,
    part_out,
    fields_ref,
    pore_ref,
    rate_ref,
    part_ref,
    occ_ref,
    cell_ref,
    send_ref,
    count_ref,
    land_ref,
    load_sem,
    state,
    natural,
    keep_turned,
    relax_turned,
    split_state,
    values,
    deposit_hot,
    total,
    hx_out,
    hy_out,
    hx,
    hy,
    axial_out,
    axial_in,
    diag_out,
    diag_in,
    send_sem,
    recv_sem,
):
    ix = lax.axis_index("gx")
    iy = lax.axis_index("gy")

    def device(move):
        return (lax.rem(ix + move[0] + nx, nx), lax.rem(iy + move[1] + ny, ny))

    def present(move):
        x, y = ix - move[0], iy - move[1]
        return (x >= 0) & (x < nx) & (y >= 0) & (y < ny)

    loads = []
    for src, dst in (
        (rate_hbm, rate_ref),
        (cell_hbm, cell_ref),
        (part_hbm, part_ref),
        (occ_hbm, occ_ref),
        (send_hbm, send_ref),
        (count_hbm, count_ref),
        (pore_hbm, pore_ref),
        (fields_hbm, fields_ref),
        (land_hbm, land_ref),
    ):
        copy = pltpu.make_async_copy(src, dst, load_sem.at[len(loads)])
        copy.start()
        loads.append(copy)

    copies = []

    def send(src, dst, move):
        k = len(copies)
        copy = pltpu.make_async_remote_copy(
            src_ref=src,
            dst_ref=dst,
            send_sem=send_sem.at[k],
            recv_sem=recv_sem.at[k],
            device_id=device(move),
            device_id_type=MESH,
        )
        copy.start()
        copies.append(copy)
        return copy

    barrier = pltpu.get_barrier_semaphore()
    for move in MOVES:
        pl.semaphore_signal(barrier, inc=1, device_id=device(move), device_id_type=MESH)

    def lanes_of(y):
        return slice(y * SLOTS, (y + 1) * SLOTS)

    def rows_of(y):
        return slice(y * CX, (y + 1) * CX)

    loads[0].wait()
    loads[1].wait()
    rate = rate_ref[...]
    keep = jnp.exp(-rate)
    relax = jnp.exp(-rate / ROT)
    lane = iota((CX, SLOTS), 1)

    keep_slot, relax_slot = [], []
    for y in range(CY):
        half = slice((y // 8) * 128, (y // 8) * 128 + 128)
        index = cell_ref[:, lanes_of(y)] + (y % 8) * CZ
        keep_slot.append(jnp.take_along_axis(keep[:, half], index, axis=1))
        relax_slot.append(jnp.take_along_axis(relax[:, half], index, axis=1))

    for copy in loads[2:6]:
        copy.wait()
    occ = occ_ref[...]
    live = [lane < occ[:, y : y + 1] for y in range(CY)]

    def turn(pieces):
        return jnp.transpose(jnp.concatenate(pieces, axis=0))

    def load_state(c):
        pieces = [jnp.where(live[y], part_ref[c, :, lanes_of(y)], 0.0) for y in range(CY)]
        if c >= 3 and c < 7:
            for y in range(CY):
                natural[c - 3, rows_of(y), :] = pieces[y]
        state[c] = turn(pieces)

    def put_split(k, value):
        high, low = split(value[:LIVE])
        rows = slice(k * LIVE, (k + 1) * LIVE)
        split_state[rows, 0:BLOCKS] = high
        split_state[rows, BLOCKS : 2 * BLOCKS] = low

    def diag_rows(ref, step):
        at = iota((8, 128), 1) // DIAG
        out = jnp.zeros((8, 128), I32)
        for d in range(4):
            row = jnp.broadcast_to(ref[step * 8 + 4 + d][:, 0:128], (8, 128))
            out = jnp.where(at == d, roll(row, d * DIAG, 1), out)
        return out[0:1]

    def slots_of(ref, step):
        slots = [ref[step * 8 + d] for d in range(4)] + [diag_rows(ref, step)]
        return jnp.concatenate(slots, axis=1)

    def send_list(step):
        slots = slots_of(send_ref, step)
        used = [
            (iota((1, CAP), 1) < count_ref[step * 8 + d]).astype(I32) for d in range(4)
        ]
        at = iota((1, 128), 1)
        ok = at < 0
        for d in range(4):
            ok = ok | ((at >= d * DIAG) & (at < d * DIAG + count_ref[step * 8 + 4 + d]))
        used.append(ok.astype(I32))
        row = jnp.where(jnp.concatenate(used, axis=1) > 0, block_row(slots), -1)
        flag = roll(jnp.broadcast_to(used[4].astype(F32), (4, 128)), 64, 1)
        return row, slots & 127, onehot_rows(row, BLOCKS), flag

    def gather(listed, first, parts):
        _, place, row_hot, flag = listed
        count = 4 * len(parts)
        for start in range(0, LIST, 256):
            stop = min(start + 256, LIST)
            n = stop - start
            hot = row_hot[:, start:stop]
            mine = iota((LIVE, n), 0) == place[:, start:stop]
            product = dot(
                split_state[first * LIVE : (first + count) * LIVE, :],
                jnp.concatenate([hot, hot], axis=0),
            )
            got = [
                jnp.sum(
                    jnp.where(mine, product[c * LIVE : (c + 1) * LIVE], 0.0),
                    axis=0,
                    keepdims=True,
                )
                for c in range(count)
            ]
            for i, part in enumerate(parts):
                four = jnp.concatenate(got[4 * i : 4 * i + 4], axis=0)
                for tile in range(start // 128, stop // 128):
                    piece = four[:, tile * 128 - start : tile * 128 - start + 128]
                    if tile < AXIAL // 128:
                        at = (tile % 3) * 128
                        axial_out[tile // 3, part, :, at : at + 128] = piece
                    else:
                        diag_out[part] = jnp.where(iota((4, 128), 1) < 64, piece, flag)

    def send_axial(first, count):
        parts = pl.ds(first, count)
        return [send(axial_out.at[d, parts], axial_in.at[d, parts], MOVES[d]) for d in range(4)]

    def send_corners(first, count):
        parts = pl.ds(first, count)
        return [
            send(diag_out.at[parts], diag_in.at[d, parts], MOVES[4 + d]) for d in range(4)
        ]

    def deposit(weight):
        for y in range(CY):
            w = weight(y)
            values[0, rows_of(y), :] = w
            for c in range(3):
                values[1 + c, rows_of(y), :] = w * natural[c, rows_of(y), :]
        own = iota((CY, FLAT), 1) // CZ == iota((CY, FLAT), 0)
        out = [[] for _ in range(4)]
        for x in range(CX):
            picked = jnp.concatenate(
                [values[c, pl.ds(x, CY, stride=CX), :] for c in range(4)], axis=0
            )
            high, low = split(picked)
            both = dot_nt(jnp.concatenate([high, low], axis=0), deposit_hot[x])
            both = both[: 4 * CY] + both[4 * CY :]
            for c in range(4):
                part = jnp.where(own, both[c * CY : (c + 1) * CY], 0.0)
                out[c].append(jnp.sum(part, axis=0, keepdims=True))
        return [jnp.concatenate(o, axis=0) for o in out]

    def pack_x(parts, shift):
        at = iota((8, FLAT), 0) // 2
        out = jnp.zeros((8, FLAT), F32)
        for i, part in enumerate(parts):
            out = jnp.where(at == i, roll(part, 2 * i - shift, 0), out)
        return out

    def pack_y(parts, shift):
        at = iota((CX, 128), 1) // 32
        out = jnp.zeros((CX, 128), F32)
        for i, part in enumerate(parts):
            out = jnp.where(at == i, roll(part, 32 * i - shift, 1), out)
        return out

    def send_halo(step):
        own = [total[step, c] for c in range(4)]
        hx_out[step, 0, 0] = pack_x([w[8:16] for w in own], 6)
        hx_out[step, 1, 0] = pack_x([w[0:8] for w in own], 0)
        hy_out[step, 0, 0] = pack_y([w[:, 128:256] for w in own], 96)
        hy_out[step, 1, 0] = pack_y([w[:, 0:128] for w in own], 0)
        if step == 0:
            for d in range(4):
                counts = [count_ref[s * 8 + d].astype(F32) for s in range(STEPS)]
                if d < 2:
                    rows = slice(8, 16) if d == 0 else slice(0, 8)
                    packed = pack_x([fluid[rows], keep[rows]], 6 if d == 0 else 0)
                    at = iota((8, FLAT), 0)
                    packed = jnp.where(at == 4, counts[0], jnp.where(at == 5, counts[1], packed))
                    hx_out[0, d, 1] = packed
                else:
                    lanes = slice(128, 256) if d == 2 else slice(0, 128)
                    packed = pack_y([fluid[:, lanes], keep[:, lanes]], 96 if d == 2 else 0)
                    at = iota((CX, 128), 1) // 32
                    packed = jnp.where(at == 2, counts[0], jnp.where(at == 3, counts[1], packed))
                    hy_out[0, d - 2, 1] = packed
            return [
                send(hx_out.at[0, 0], hx.at[0, 0], MOVES[0]),
                send(hx_out.at[0, 1], hx.at[0, 1], MOVES[1]),
                send(hy_out.at[0, 0], hy.at[0, 0], MOVES[2]),
                send(hy_out.at[0, 1], hy.at[0, 1], MOVES[3]),
            ]
        return [
            send(hx_out.at[step, 0, 0], hx.at[step, 0, 0], MOVES[0]),
            send(hx_out.at[step, 1, 0], hx.at[step, 1, 0], MOVES[1]),
            send(hy_out.at[step, 0, 0], hy.at[step, 0, 0], MOVES[2]),
            send(hy_out.at[step, 1, 0], hy.at[step, 1, 0], MOVES[3]),
        ]

    def ring_x(own, low, high, i):
        at = iota((8, FLAT), 0)
        low = jnp.where((at >= 6) & present(MOVES[0]), roll(low, 6 - 2 * i, 0), 0.0)
        edge = jnp.where((at < 2) & present(MOVES[1]), roll(high, -2 * i, 0), low)
        return jnp.concatenate([own, edge], axis=0)

    def ring_y(own, low, high, i):
        at = iota((CX, 128), 1)
        low = jnp.where((at >= 96) & present(MOVES[2]), roll(low, 96 - 32 * i, 1), 0.0)
        edge = jnp.where((at < 32) & present(MOVES[3]), roll(high, -32 * i, 1), low)
        return jnp.concatenate([own, edge], axis=1)

    def move_x(w, k):
        return roll(w, -k, 0)

    def move_y(w, k):
        return roll(w, -k * CZ, 1)

    zpos = iota((CX, FLAT), 1) % CZ

    def move_z(w, k):
        inside = (zpos + k >= 0) & (zpos + k < CZ)
        return jnp.where(inside, roll(w, -k, 1), 0.0)

    def coefs():
        def one(f, k, move):
            return f * move(f, 1) * (1.0 - 0.5 * (k + move(k, 1)))

        ex = [(hx[0, 0, 1], hx[0, 1, 1], i) for i in range(2)]
        ey = [(hy[0, 0, 1], hy[0, 1, 1], i) for i in range(2)]
        x = one(ring_x(fluid, *ex[0]), ring_x(keep, *ex[1]), move_x)
        y = one(ring_y(fluid, *ey[0]), ring_y(keep, *ey[1]), move_y)
        return x, y, one(fluid, keep, move_z)

    def divergence(step, coef):
        own = [total[step, c] for c in range(4)]
        xs = [ring_x(own[c], hx[step, 0, 0], hx[step, 1, 0], c) for c in range(4)]
        ys = [ring_y(own[c], hy[step, 0, 0], hy[step, 1, 0], c) for c in range(4)]
        fx = flux_of(xs, coef[0], 0, move_x)
        fy = flux_of(ys, coef[1], 1, move_y)
        fz = flux_of(own, coef[2], 2, move_z)
        out = []
        for c in range(4):
            dx = (fx[c] - move_x(fx[c], -1))[:CX]
            dy = (fy[c] - move_y(fy[c], -1))[:, :FLAT]
            out.append(dx + dy + (fz[c] - move_z(fz[c], -1)))
        return out

    def collide(c, value):
        if c < 3:
            return value + COURANT * state[3 + c]
        if c == 6:
            return value * keep_turned[...]
        return 1.0 + (value - 1.0) * relax_turned[...]

    def arrived(step, rows):
        at = iota((1, CAP), 1).astype(F32)
        fits = []
        for d in range(4):
            if d < 2:
                count = hx[0, d, 1][4 + step : 5 + step, 0:1]
            else:
                count = hy[0, d - 2, 1][0:1, 64 + 32 * step : 65 + 32 * step]
            fits.append((at < jnp.broadcast_to(count, (1, CAP))) & present(MOVES[d]))
        lane = iota((4, 128), 1)
        corners = {}
        for part in sorted({part for part, _ in rows}):
            got = jnp.zeros((4, 128), F32)
            for d in range(4):
                mine = (lane % 64) // DIAG == d
                got = jnp.where(mine & present(MOVES[4 + d]), diag_in[d, part], got)
            corners[part] = got
        got = corners[rows[0][0]]
        flag = (roll(got, 64, 1) > 0.5) & (lane < 64)
        fits.append(flag[0:1])
        fit = jnp.concatenate([f.astype(F32) for f in fits], axis=1) > 0.5
        out = []
        for part, at in rows:
            pieces = [axial_in[d, part, at : at + 1, :] for d in range(4)]
            pieces.append(corners[part][at : at + 1])
            out.append(jnp.where(fit, jnp.concatenate(pieces, axis=1), 0.0))
        return out, fit

    keep_turned[...] = turn(keep_slot)
    for c in (6, 3, 4, 5):
        load_state(c)
    weight = collide(6, state[6])
    state[6] = weight
    put_split(0, weight)
    for c in range(3):
        put_split(1 + c, state[3 + c])
    listed = [send_list(0)]
    gather(listed[0], 0, [0])
    pl.semaphore_wait(barrier, len(MOVES))
    first = send_axial(0, 1) + send_corners(0, 1)

    for x in range(CX):
        for y in range(CY):
            mine = iota((CZ, SLOTS), 0) == jnp.broadcast_to(
                cell_ref[x : x + 1, lanes_of(y)], (CZ, SLOTS)
            )
            deposit_hot[x, y * CZ : (y + 1) * CZ, :] = jnp.where(mine, 1.0, 0.0).astype(BF16)
    moments = deposit(lambda y: natural[3, rows_of(y), :])
    for copy in loads[6:]:
        copy.wait()
    fluid = pore_ref[...].astype(F32)
    for c in range(4):
        total[0, c] = (fields_ref[c] + moments[c]) * fluid
    halo = send_halo(0)

    relax_turned[...] = turn(relax_slot)
    for k, c in enumerate((0, 1, 2, 7)):
        load_state(c)
        value = collide(c, state[c])
        put_split(9 + k, value)
        value = collide(c, value)
        put_split(5 + k, value)
        state[c] = value
    weight = collide(6, state[6])
    put_split(4, weight)
    state[6] = weight
    listed.append(send_list(1))
    gather(listed[0], 9, [1])
    second = send_axial(1, 1)
    gather(listed[1], 1, [2, 3])
    late = send_axial(2, 2) + send_corners(1, 3)

    left = [
        dot_nt(onehot_rows(place, LIVE), row_hot) > 0.5 for _, place, row_hot, _ in listed
    ]
    gone = jnp.transpose(
        jnp.concatenate(
            [left[0].astype(F32), jnp.zeros((SLOTS - LIVE, BLOCKS), F32)], axis=0
        )
    )
    stay = deposit(
        lambda y: jnp.where(
            gone[rows_of(y)] > 0.5, 0.0, natural[3, rows_of(y), :] * keep_slot[y]
        )
    )
    for c in range(8):
        rest = 1.0 - relax_turned[:LIVE] if c == 7 else 0.0
        value = jnp.where(left[0], rest, state[c, :LIVE])
        state[c, :LIVE] = jnp.where(left[1], 0.0, value)

    slots = [slots_of(land_ref, step) for step in range(STEPS)]
    place_hots = [onehot_rows((t & 127) - DEAD, SPAN) for t in slots]
    row = block_row(slots[0])
    row_hots = [onehot_rows(block_row(t), BLOCKS) for t in slots]
    cell_all = turn([cell_ref[:, lanes_of(y)].astype(F32) for y in range(CY)])
    found = dot(cell_all[DEAD:].astype(BF16), row_hots[0])
    z = jnp.sum(
        jnp.where(iota((SPAN, LIST), 0) == (slots[0] & 127) - DEAD, found, 0.0),
        axis=0,
        keepdims=True,
    )
    flat_cell = (row >> 4).astype(F32) * CZ + z
    cell_hot = jnp.where(
        iota((FLAT, LIST), 0).astype(F32) == flat_cell, 1.0, 0.0
    ).astype(BF16)
    x_mine = iota((CX, LIST), 0) == (row & 15)
    table = jnp.concatenate([*split(keep), *split(relax)], axis=0)
    factors = dot(table, cell_hot)

    def factor(k):
        both = factors[2 * k * CX : (2 * k + 1) * CX] + factors[(2 * k + 1) * CX : (2 * k + 2) * CX]
        return jnp.sum(jnp.where(x_mine, both, 0.0), axis=0, keepdims=True)

    keep_land, relax_land = factor(0), factor(1)

    for copy in first + halo:
        copy.wait()
    (w, vx, vy, vz), fit = arrived(0, [(0, k) for k in range(4)])
    highs, lows = [], []
    for value in (w, w * vx, w * vy, w * vz):
        high, low = split(jnp.where(x_mine, value, 0.0))
        highs.append(high)
        lows.append(low)
    landed = dot_nt(jnp.concatenate(highs + lows, axis=0), cell_hot)
    landed = landed[: 4 * CX] + landed[4 * CX :]
    coef = coefs()
    div = divergence(0, coef)
    fields = [
        fields_ref[c] - COURANT * div[c] + (1.0 - keep) * moments[c] for c in range(4)
    ]
    moments = [stay[c] + landed[c * CX : (c + 1) * CX] for c in range(4)]
    for c in range(4):
        total[1, c] = (fields[c] + moments[c]) * fluid
    halo = send_halo(1)

    def masked(step, fit):
        hot = place_hots[step] * fit.astype(F32).astype(BF16)
        return dot_nt(hot, row_hots[step]) > 0.5

    def land(step, taken, comps, news):
        parts = []
        for new in news:
            high, low = split(new)
            parts += [place_hots[step] * high, place_hots[step] * low]
        got = dot_nt(jnp.concatenate(parts, axis=0), row_hots[step])
        for i, c in enumerate(comps):
            new = got[2 * i * SPAN : (2 * i + 1) * SPAN]
            new = new + got[(2 * i + 1) * SPAN : (2 * i + 2) * SPAN]
            state[c, DEAD:] = jnp.where(taken, 0.0, state[c, DEAD:]) + new

    taken = masked(0, fit)
    land(0, taken, (6, 3, 4, 5), (w * keep_land, vx, vy, vz))
    for copy in second + late[4:]:
        copy.wait()
    (px, py, pz, rot), _ = arrived(0, [(1, k) for k in range(4)])
    land(
        0,
        taken,
        (0, 1, 2, 7),
        (
            px + COURANT * vx,
            py + COURANT * vy,
            pz + COURANT * vz,
            jnp.where(fit, 1.0 + (rot - 1.0) * relax_land, 0.0),
        ),
    )
    for copy in late[:4]:
        copy.wait()
    for part, comps in ((2, (3, 4, 5, 6)), (3, (0, 1, 2, 7))):
        news, fit = arrived(1, [(part, k) for k in range(4)])
        if part == 2:
            taken = masked(1, fit)
        land(1, taken, comps, news)
        for c in comps:
            whole = jnp.transpose(state[c])
            for y in range(CY):
                part_out[c, :, lanes_of(y)] = whole[rows_of(y)]
    for copy in halo:
        copy.wait()
    div = divergence(1, coef)
    for c in range(4):
        fields_out[c] = fields[c] - COURANT * div[c] + (1.0 - keep) * moments[c]


def solution(mesh):
    nx, ny = mesh.shape["gx"], mesh.shape["gy"]

    def body(fields, pore, rate, particles, occupancy, slot_cell, send_slot, send_count, land_slot):
        vmem = pl.BlockSpec(memory_space=pltpu.VMEM)
        hbm = pl.BlockSpec(memory_space=pltpu.HBM)
        copies = 8 * STEPS + 4 + 4 * STEPS

        def run(*refs):
            kernel(nx, ny, *refs)

        return pl.pallas_call(
            run,
            out_shape=(
                jax.ShapeDtypeStruct(fields.shape, F32),
                jax.ShapeDtypeStruct(particles.shape, F32),
            ),
            in_specs=[hbm] * 9,
            out_specs=(vmem, vmem),
            scratch_shapes=[
                pltpu.VMEM(fields.shape, F32),
                pltpu.VMEM(pore.shape, I32),
                pltpu.VMEM(rate.shape, F32),
                pltpu.VMEM(particles.shape, F32),
                pltpu.VMEM(occupancy.shape, I32),
                pltpu.VMEM(slot_cell.shape, I32),
                pltpu.VMEM(send_slot.shape, I32),
                pltpu.SMEM((STEPS * 8,), I32),
                pltpu.VMEM(land_slot.shape, I32),
                pltpu.SemaphoreType.DMA((9,)),
                pltpu.VMEM((8, SLOTS, BLOCKS), F32),
                pltpu.VMEM((4, BLOCKS, SLOTS), F32),
                pltpu.VMEM((SLOTS, BLOCKS), F32),
                pltpu.VMEM((SLOTS, BLOCKS), F32),
                pltpu.VMEM((13 * LIVE, 2 * BLOCKS), BF16),
                pltpu.VMEM((4, BLOCKS, SLOTS), F32),
                pltpu.VMEM((CX, FLAT, SLOTS), BF16),
                pltpu.VMEM((STEPS, 4, CX, FLAT), F32),
                pltpu.VMEM((STEPS, 2, 2, 8, FLAT), F32),
                pltpu.VMEM((STEPS, 2, 2, CX, 128), F32),
                pltpu.VMEM((STEPS, 2, 2, 8, FLAT), F32),
                pltpu.VMEM((STEPS, 2, 2, CX, 128), F32),
                pltpu.VMEM((4, 4, 4, CAP), F32),
                pltpu.VMEM((4, 4, 4, CAP), F32),
                pltpu.VMEM((4, 4, 128), F32),
                pltpu.VMEM((4, 4, 4, 128), F32),
                pltpu.SemaphoreType.DMA((copies,)),
                pltpu.SemaphoreType.DMA((copies,)),
            ],
            compiler_params=pltpu.CompilerParams(
                collective_id=0, has_side_effects=True, vmem_limit_bytes=48 << 20
            ),
        )(
            *[
                pltpu.with_memory_space_constraint(x, pltpu.HBM)
                for x in (
                    fields,
                    pore,
                    rate,
                    particles,
                    occupancy,
                    slot_cell,
                    send_slot,
                    send_count.reshape(STEPS * 8),
                    land_slot,
                )
            ]
        )

    return jax.shard_map(
        body,
        mesh=mesh,
        in_specs=(
            P(None, "gx", "gy"),
            P("gx", "gy"),
            P("gx", "gy"),
            P(None, "gx", "gy"),
            P("gx", "gy"),
            P("gx", "gy"),
            P(None, "gx", "gy"),
            P(None, "gx", "gy"),
            P(None, "gx", "gy"),
        ),
        out_specs=(P(None, "gx", "gy"), P(None, "gx", "gy")),
        check_vma=False,
    )
```

```python
import jax
import jax.numpy as jnp
from jax import lax
from jax.experimental import pallas as pl
from jax.experimental.pallas import tpu as pltpu
from jax.sharding import PartitionSpec as P

CX = 16
CY = 16
CZ = 16
SLOTS = 128
STEPS = 2
CAP = 384
DIAG = 16
BLOCKS = CX * CY
FLAT = CY * CZ
AXIAL = 4 * CAP
LIST = AXIAL + 128
LIVE = 96
DEAD = 32
SPAN = SLOTS - DEAD
COURANT = 0.25
ROT = 4.0
MOVES = ((1, 0), (-1, 0), (0, 1), (0, -1), (1, 1), (1, -1), (-1, 1), (-1, -1))
F32 = jnp.float32
BF16 = jnp.bfloat16
I32 = jnp.int32
MESH = pl.DeviceIdType.MESH


def iota(shape, dim):
    return lax.broadcasted_iota(I32, shape, dim)


def split(x):
    high = (x * 0.995).astype(BF16)
    low = (x - high.astype(F32)).astype(BF16)
    return high, low


def dot(a, b):
    return lax.dot_general(a, b, (((1,), (0,)), ((), ())), preferred_element_type=F32)


def dot_nt(a, b):
    return lax.dot_general(a, b, (((1,), (1,)), ((), ())), preferred_element_type=F32)


def roll(x, by, axis):
    return pltpu.roll(x, by % x.shape[axis], axis)


def onehot_rows(row, size):
    n = row.shape[1]
    return jnp.where(iota((size, n), 0) == row, 1.0, 0.0).astype(BF16)


def block_row(slot):
    block = slot >> 7
    return (block & 15) * CX + (block >> 4)


def flux_of(comps, coef, axis_n, move):
    nxt = [move(w, 1) for w in comps]

    def centred(w, w_next):
        return 7.0 / 12.0 * (w + w_next) - 1.0 / 12.0 * (move(w, -1) + move(w, 2))

    out = []
    for c in range(4):
        value = -0.5 * (nxt[c] - comps[c])
        if c == 0:
            value = value + centred(comps[1 + axis_n], nxt[1 + axis_n])
        if c == 1 + axis_n:
            value = value + centred(comps[0], nxt[0])
        out.append(coef * value)
    return out


def kernel(
    nx,
    ny,
    fields_hbm,
    pore_hbm,
    rate_hbm,
    part_hbm,
    occ_hbm,
    cell_hbm,
    send_hbm,
    count_hbm,
    land_hbm,
    fields_out,
    part_out,
    fields_ref,
    pore_ref,
    rate_ref,
    part_ref,
    occ_ref,
    cell_ref,
    send_ref,
    count_ref,
    land_ref,
    load_sem,
    state,
    natural,
    keep_turned,
    relax_turned,
    split_state,
    values,
    deposit_hot,
    total,
    hx_out,
    hy_out,
    hx,
    hy,
    axial_out,
    axial_in,
    diag_out,
    diag_in,
    send_sem,
    recv_sem,
):
    ix = lax.axis_index("gx")
    iy = lax.axis_index("gy")

    def device(move):
        return (lax.rem(ix + move[0] + nx, nx), lax.rem(iy + move[1] + ny, ny))

    def present(move):
        x, y = ix - move[0], iy - move[1]
        return (x >= 0) & (x < nx) & (y >= 0) & (y < ny)

    loads = []
    for src, dst in (
        (rate_hbm, rate_ref),
        (cell_hbm, cell_ref),
        (part_hbm.at[3:7], part_ref.at[3:7]),
        (occ_hbm, occ_ref),
        (send_hbm, send_ref),
        (count_hbm, count_ref),
        (part_hbm.at[0:3], part_ref.at[0:3]),
        (part_hbm.at[7:8], part_ref.at[7:8]),
        (pore_hbm, pore_ref),
        (fields_hbm, fields_ref),
        (land_hbm, land_ref),
    ):
        copy = pltpu.make_async_copy(src, dst, load_sem.at[len(loads)])
        copy.start()
        loads.append(copy)

    copies = []

    def send(src, dst, move):
        k = len(copies)
        copy = pltpu.make_async_remote_copy(
            src_ref=src,
            dst_ref=dst,
            send_sem=send_sem.at[k],
            recv_sem=recv_sem.at[k],
            device_id=device(move),
            device_id_type=MESH,
        )
        copy.start()
        copies.append(copy)
        return copy

    barrier = pltpu.get_barrier_semaphore()
    for move in MOVES:
        pl.semaphore_signal(barrier, inc=1, device_id=device(move), device_id_type=MESH)

    def lanes_of(y):
        return slice(y * SLOTS, (y + 1) * SLOTS)

    def rows_of(y):
        return slice(y * CX, (y + 1) * CX)

    loads[0].wait()
    loads[1].wait()
    rate = rate_ref[...]
    keep = jnp.exp(-rate)
    relax = jnp.exp(-rate / ROT)
    lane = iota((CX, SLOTS), 1)

    keep_slot, relax_slot = [], []
    for y in range(CY):
        half = slice((y // 8) * 128, (y // 8) * 128 + 128)
        index = cell_ref[:, lanes_of(y)] + (y % 8) * CZ
        keep_slot.append(jnp.take_along_axis(keep[:, half], index, axis=1))
        relax_slot.append(jnp.take_along_axis(relax[:, half], index, axis=1))

    for copy in loads[2:6]:
        copy.wait()
    occ = occ_ref[...]
    live = [lane < occ[:, y : y + 1] for y in range(CY)]

    def turn(pieces):
        return jnp.transpose(jnp.concatenate(pieces, axis=0))

    def load_state(c):
        pieces = [jnp.where(live[y], part_ref[c, :, lanes_of(y)], 0.0) for y in range(CY)]
        if c >= 3 and c < 7:
            for y in range(CY):
                natural[c - 3, rows_of(y), :] = pieces[y]
        state[c] = turn(pieces)

    def put_split(k, value):
        high, low = split(value[:LIVE])
        rows = slice(k * LIVE, (k + 1) * LIVE)
        split_state[rows, 0:BLOCKS] = high
        split_state[rows, BLOCKS : 2 * BLOCKS] = low

    def diag_rows(ref, step):
        at = iota((8, 128), 1) // DIAG
        out = jnp.zeros((8, 128), I32)
        for d in range(4):
            row = jnp.broadcast_to(ref[step * 8 + 4 + d][:, 0:128], (8, 128))
            out = jnp.where(at == d, roll(row, d * DIAG, 1), out)
        return out[0:1]

    def slots_of(ref, step):
        slots = [ref[step * 8 + d] for d in range(4)] + [diag_rows(ref, step)]
        return jnp.concatenate(slots, axis=1)

    def send_list(step):
        slots = slots_of(send_ref, step)
        used = [
            (iota((1, CAP), 1) < count_ref[step * 8 + d]).astype(I32) for d in range(4)
        ]
        at = iota((1, 128), 1)
        ok = at < 0
        for d in range(4):
            ok = ok | ((at >= d * DIAG) & (at < d * DIAG + count_ref[step * 8 + 4 + d]))
        used.append(ok.astype(I32))
        row = jnp.where(jnp.concatenate(used, axis=1) > 0, block_row(slots), -1)
        flag = jnp.broadcast_to(used[4].astype(F32), (8, 128))
        return row, slots & 127, onehot_rows(row, BLOCKS), flag

    def gather(listed, first, parts, starts):
        _, place, row_hot, _ = listed
        count = 4 * len(parts)
        for start in starts:
            stop = min(start + 256, LIST)
            n = stop - start
            hot = row_hot[:, start:stop]
            mine = iota((LIVE, n), 0) == place[:, start:stop]
            product = dot(
                split_state[first * LIVE : (first + count) * LIVE, :],
                jnp.concatenate([hot, hot], axis=0),
            )
            got = [
                jnp.sum(
                    jnp.where(mine, product[c * LIVE : (c + 1) * LIVE], 0.0),
                    axis=0,
                    keepdims=True,
                )
                for c in range(count)
            ]
            for i, part in enumerate(parts):
                four = jnp.concatenate(got[4 * i : 4 * i + 4], axis=0)
                for tile in range(start // 128, stop // 128):
                    piece = four[:, tile * 128 - start : tile * 128 - start + 128]
                    if tile < AXIAL // 128:
                        at = (tile % 3) * 128
                        axial_out[tile // 3, part, :, at : at + 128] = piece
                    else:
                        diag_out[part] = piece

    def send_axial(first, count):
        parts = pl.ds(first, count)
        return [send(axial_out.at[d, parts], axial_in.at[d, parts], MOVES[d]) for d in (2, 3, 0, 1)]

    def send_corners(first, count):
        parts = pl.ds(first, count)
        return [
            send(diag_out.at[parts], diag_in.at[d, parts], MOVES[4 + d]) for d in range(4)
        ]

    def deposit(weight):
        for y in range(CY):
            w = weight(y)
            values[0, rows_of(y), :] = w
            for c in range(3):
                values[1 + c, rows_of(y), :] = w * natural[c, rows_of(y), :]
        own = iota((CY, FLAT), 1) // CZ == iota((CY, FLAT), 0)
        out = [[] for _ in range(4)]
        for x in range(CX):
            picked = jnp.concatenate(
                [values[c, pl.ds(x, CY, stride=CX), :] for c in range(4)], axis=0
            )
            high, low = split(picked)
            both = dot_nt(jnp.concatenate([high, low], axis=0), deposit_hot[x])
            both = both[: 4 * CY] + both[4 * CY :]
            for c in range(4):
                part = jnp.where(own, both[c * CY : (c + 1) * CY], 0.0)
                out[c].append(jnp.sum(part, axis=0, keepdims=True))
        return [jnp.concatenate(o, axis=0) for o in out]

    def pack_x(parts, shift):
        at = iota((8, FLAT), 0) // 2
        out = jnp.zeros((8, FLAT), F32)
        for i, part in enumerate(parts):
            out = jnp.where(at == i, roll(part, 2 * i - shift, 0), out)
        return out

    def pack_y(parts, shift):
        at = iota((CX, 128), 1) // 32
        out = jnp.zeros((CX, 128), F32)
        for i, part in enumerate(parts):
            out = jnp.where(at == i, roll(part, 32 * i - shift, 1), out)
        return out

    def send_halo(step):
        own = [total[step, c] for c in range(4)]
        hx_out[step, 0, 0] = pack_x([w[8:16] for w in own], 6)
        hx_out[step, 1, 0] = pack_x([w[0:8] for w in own], 0)
        hy_out[step, 0, 0] = pack_y([w[:, 128:256] for w in own], 96)
        hy_out[step, 1, 0] = pack_y([w[:, 0:128] for w in own], 0)
        if step == 0:
            for d in range(4):
                counts = [count_ref[s * 8 + d].astype(F32) for s in range(STEPS)]
                if d < 2:
                    rows = slice(8, 16) if d == 0 else slice(0, 8)
                    packed = pack_x([fluid[rows], keep[rows]], 6 if d == 0 else 0)
                    at = iota((8, FLAT), 0)
                    packed = jnp.where(at == 4, counts[0], jnp.where(at == 5, counts[1], packed))
                    hx_out[0, d, 1] = packed
                else:
                    lanes = slice(128, 256) if d == 2 else slice(0, 128)
                    packed = pack_y([fluid[:, lanes], keep[:, lanes]], 96 if d == 2 else 0)
                    at = iota((CX, 128), 1) // 32
                    packed = jnp.where(at == 2, counts[0], jnp.where(at == 3, counts[1], packed))
                    hy_out[0, d - 2, 1] = packed
            return [
                send(hy_out.at[0, 0], hy.at[0, 0], MOVES[2]),
                send(hy_out.at[0, 1], hy.at[0, 1], MOVES[3]),
                send(hx_out.at[0, 0], hx.at[0, 0], MOVES[0]),
                send(hx_out.at[0, 1], hx.at[0, 1], MOVES[1]),
            ]
        return [
            send(hy_out.at[step, 0, 0], hy.at[step, 0, 0], MOVES[2]),
            send(hy_out.at[step, 1, 0], hy.at[step, 1, 0], MOVES[3]),
            send(hx_out.at[step, 0, 0], hx.at[step, 0, 0], MOVES[0]),
            send(hx_out.at[step, 1, 0], hx.at[step, 1, 0], MOVES[1]),
        ]

    def ring_x(own, low, high, i):
        at = iota((8, FLAT), 0)
        low = jnp.where((at >= 6) & present(MOVES[0]), roll(low, 6 - 2 * i, 0), 0.0)
        edge = jnp.where((at < 2) & present(MOVES[1]), roll(high, -2 * i, 0), low)
        return jnp.concatenate([own, edge], axis=0)

    def ring_y(own, low, high, i):
        at = iota((CX, 128), 1)
        low = jnp.where((at >= 96) & present(MOVES[2]), roll(low, 96 - 32 * i, 1), 0.0)
        edge = jnp.where((at < 32) & present(MOVES[3]), roll(high, -32 * i, 1), low)
        return jnp.concatenate([own, edge], axis=1)

    def move_x(w, k):
        return roll(w, -k, 0)

    def move_y(w, k):
        return roll(w, -k * CZ, 1)

    zpos = iota((CX, FLAT), 1) % CZ

    def move_z(w, k):
        inside = (zpos + k >= 0) & (zpos + k < CZ)
        return jnp.where(inside, roll(w, -k, 1), 0.0)

    def coefs():
        def one(f, k, move):
            return f * move(f, 1) * (1.0 - 0.5 * (k + move(k, 1)))

        ex = [(hx[0, 0, 1], hx[0, 1, 1], i) for i in range(2)]
        ey = [(hy[0, 0, 1], hy[0, 1, 1], i) for i in range(2)]
        x = one(ring_x(fluid, *ex[0]), ring_x(keep, *ex[1]), move_x)
        y = one(ring_y(fluid, *ey[0]), ring_y(keep, *ey[1]), move_y)
        return x, y, one(fluid, keep, move_z)

    def divergence(step, coef):
        own = [total[step, c] for c in range(4)]
        xs = [ring_x(own[c], hx[step, 0, 0], hx[step, 1, 0], c) for c in range(4)]
        ys = [ring_y(own[c], hy[step, 0, 0], hy[step, 1, 0], c) for c in range(4)]
        fx = flux_of(xs, coef[0], 0, move_x)
        fy = flux_of(ys, coef[1], 1, move_y)
        fz = flux_of(own, coef[2], 2, move_z)
        out = []
        for c in range(4):
            dx = (fx[c] - move_x(fx[c], -1))[:CX]
            dy = (fy[c] - move_y(fy[c], -1))[:, :FLAT]
            out.append(dx + dy + (fz[c] - move_z(fz[c], -1)))
        return out

    def collide(c, value):
        if c < 3:
            return value + COURANT * state[3 + c]
        if c == 6:
            return value * keep_turned[...]
        return 1.0 + (value - 1.0) * relax_turned[...]

    def fit_list(step):
        at = iota((1, CAP), 1).astype(F32)
        fits = []
        for d in range(4):
            if d < 2:
                count = hx[0, d, 1][4 + step : 5 + step, 0:1]
            else:
                count = hy[0, d - 2, 1][0:1, 64 + 32 * step : 65 + 32 * step]
            fits.append((at < jnp.broadcast_to(count, (1, CAP))) & present(MOVES[d]))
        lane = iota((4, 128), 1)
        got = jnp.zeros((4, 128), F32)
        for d in range(4):
            mine = (lane % 64) // DIAG == d
            got = jnp.where(mine & present(MOVES[4 + d]), diag_in[d, 0], got)
        flag = (roll(got, 64, 1) > 0.5) & (lane < 64)
        fits.append(flag[2 * step : 2 * step + 1])
        return jnp.concatenate([f.astype(F32) for f in fits], axis=1) > 0.5

    def arrived(fit, rows):
        lane = iota((4, 128), 1)
        corners = {}
        for part in sorted({part for part, _ in rows}):
            got = jnp.zeros((4, 128), F32)
            for d in range(4):
                mine = (lane % 64) // DIAG == d
                got = jnp.where(mine & present(MOVES[4 + d]), diag_in[d, part], got)
            corners[part] = got
        out = []
        for part, at in rows:
            pieces = [axial_in[d, part, at : at + 1, :] for d in range(4)]
            pieces.append(corners[part][at : at + 1])
            out.append(jnp.where(fit, jnp.concatenate(pieces, axis=1), 0.0))
        return out

    keep_turned[...] = turn(keep_slot)
    for c in (6, 3, 4, 5):
        load_state(c)
    weight = collide(6, state[6])
    state[6] = weight
    put_split(0, weight)
    for c in range(3):
        put_split(1 + c, state[3 + c])
    listed = [send_list(step) for step in range(STEPS)]
    axial_starts = list(range(0, AXIAL, 256))
    gather(listed[0], 0, [0], axial_starts + [AXIAL])
    flags = jnp.where(iota((8, 128), 0) < 2, listed[0][3], listed[1][3])
    flags = roll(flags, 64, 1)[0:4]
    diag_out[0] = jnp.where(iota((4, 128), 1) < 64, diag_out[0], flags)

    for x in range(CX):
        for y in range(CY):
            mine = iota((CZ, SLOTS), 0) == jnp.broadcast_to(
                cell_ref[x : x + 1, lanes_of(y)], (CZ, SLOTS)
            )
            deposit_hot[x, y * CZ : (y + 1) * CZ, :] = jnp.where(mine, 1.0, 0.0).astype(BF16)
    moments = deposit(lambda y: natural[3, rows_of(y), :])
    for copy in loads[8:]:
        copy.wait()
    fluid = pore_ref[...].astype(F32)
    for c in range(4):
        total[0, c] = (fields_ref[c] + moments[c]) * fluid
    pl.semaphore_wait(barrier, len(MOVES))
    first = send_corners(0, 1) + send_axial(0, 1)
    halo = send_halo(0)

    for copy in loads[6:8]:
        copy.wait()
    relax_turned[...] = turn(relax_slot)
    for k, c in enumerate((0, 1, 2, 7)):
        load_state(c)
        value = collide(c, state[c])
        put_split(9 + k, value)
        value = collide(c, value)
        put_split(5 + k, value)
        state[c] = value
    weight = collide(6, state[6])
    put_split(4, weight)
    state[6] = weight
    gather(listed[0], 9, [1], [AXIAL])
    gather(listed[1], 1, [2, 3], [AXIAL])
    gather(listed[0], 9, [1], axial_starts)
    late = [send_corners(1, 3) + send_axial(1, 1)]
    gather(listed[1], 1, [2], axial_starts)
    late.append(send_axial(2, 1))
    gather(listed[1], 5, [3], axial_starts)
    late.append(send_axial(3, 1))

    left = [
        dot_nt(onehot_rows(place, LIVE), row_hot) > 0.5 for _, place, row_hot, _ in listed
    ]
    gone = jnp.transpose(
        jnp.concatenate(
            [left[0].astype(F32), jnp.zeros((SLOTS - LIVE, BLOCKS), F32)], axis=0
        )
    )
    stay = deposit(
        lambda y: jnp.where(
            gone[rows_of(y)] > 0.5, 0.0, natural[3, rows_of(y), :] * keep_slot[y]
        )
    )
    slots = [slots_of(land_ref, step) for step in range(STEPS)]
    place_hots = [onehot_rows((t & 127) - DEAD, SPAN) for t in slots]
    row = block_row(slots[0])
    row_hots = [onehot_rows(block_row(t), BLOCKS) for t in slots]
    cell_all = turn([cell_ref[:, lanes_of(y)].astype(F32) for y in range(CY)])
    found = dot(cell_all[DEAD:].astype(BF16), row_hots[0])
    z = jnp.sum(
        jnp.where(iota((SPAN, LIST), 0) == (slots[0] & 127) - DEAD, found, 0.0),
        axis=0,
        keepdims=True,
    )
    flat_cell = (row >> 4).astype(F32) * CZ + z
    cell_hot = jnp.where(
        iota((FLAT, LIST), 0).astype(F32) == flat_cell, 1.0, 0.0
    ).astype(BF16)
    x_mine = iota((CX, LIST), 0) == (row & 15)
    table = jnp.concatenate([*split(keep), *split(relax)], axis=0)
    factors = dot(table, cell_hot)

    def factor(k):
        both = factors[2 * k * CX : (2 * k + 1) * CX] + factors[(2 * k + 1) * CX : (2 * k + 2) * CX]
        return jnp.sum(jnp.where(x_mine, both, 0.0), axis=0, keepdims=True)

    keep_land, relax_land = factor(0), factor(1)

    for copy in first + halo:
        copy.wait()
    fit = [fit_list(step) for step in range(STEPS)]
    w, vx, vy, vz = arrived(fit[0], [(0, k) for k in range(4)])
    highs, lows = [], []
    for value in (w, w * vx, w * vy, w * vz):
        high, low = split(jnp.where(x_mine, value, 0.0))
        highs.append(high)
        lows.append(low)
    landed = dot_nt(jnp.concatenate(highs + lows, axis=0), cell_hot)
    landed = landed[: 4 * CX] + landed[4 * CX :]
    coef = coefs()
    div = divergence(0, coef)
    fields = [
        fields_ref[c] - COURANT * div[c] + (1.0 - keep) * moments[c] for c in range(4)
    ]
    moments = [stay[c] + landed[c * CX : (c + 1) * CX] for c in range(4)]
    for c in range(4):
        total[1, c] = (fields[c] + moments[c]) * fluid
    halo = send_halo(1)

    for c in range(8):
        rest = 1.0 - relax_turned[:LIVE] if c == 7 else 0.0
        value = jnp.where(left[0], rest, state[c, :LIVE])
        state[c, :LIVE] = jnp.where(left[1], 0.0, value)

    def land(step, comps, news):
        parts = []
        for new in news:
            high, low = split(new)
            parts += [place_hots[step] * high, place_hots[step] * low]
        if 7 in comps:
            parts.append(place_hots[step] * fit[step].astype(F32).astype(BF16))
        got = dot_nt(jnp.concatenate(parts, axis=0), row_hots[step])
        for i, c in enumerate(comps):
            new = got[2 * i * SPAN : (2 * i + 1) * SPAN]
            new = new + got[(2 * i + 1) * SPAN : (2 * i + 2) * SPAN]
            before = state[c, DEAD:]
            if c == 7:
                before = jnp.where(got[8 * SPAN :] > 0.5, 0.0, before)
            state[c, DEAD:] = before + new

    land(0, (6, 3, 4, 5), (w * keep_land, vx, vy, vz))
    for copy in late[0]:
        copy.wait()
    px, py, pz, rot = arrived(fit[0], [(1, k) for k in range(4)])
    land(
        0,
        (0, 1, 2, 7),
        (
            px + COURANT * vx,
            py + COURANT * vy,
            pz + COURANT * vz,
            jnp.where(fit[0], 1.0 + (rot - 1.0) * relax_land, 0.0),
        ),
    )
    for part, comps in ((2, (3, 4, 5, 6)), (3, (0, 1, 2, 7))):
        for copy in late[part - 1]:
            copy.wait()
        land(1, comps, arrived(fit[1], [(part, k) for k in range(4)]))
        for c in comps:
            whole = jnp.transpose(state[c])
            for y in range(CY):
                part_out[c, :, lanes_of(y)] = whole[rows_of(y)]
    for copy in halo:
        copy.wait()
    div = divergence(1, coef)
    for c in range(4):
        fields_out[c] = fields[c] - COURANT * div[c] + (1.0 - keep) * moments[c]


def solution(mesh):
    nx, ny = mesh.shape["gx"], mesh.shape["gy"]

    def body(fields, pore, rate, particles, occupancy, slot_cell, send_slot, send_count, land_slot):
        vmem = pl.BlockSpec(memory_space=pltpu.VMEM)
        hbm = pl.BlockSpec(memory_space=pltpu.HBM)
        copies = 8 * STEPS + 8 + 4 * STEPS

        def run(*refs):
            kernel(nx, ny, *refs)

        results = pl.pallas_call(
            run,
            out_shape=(
                jax.ShapeDtypeStruct(fields.shape, F32),
                jax.ShapeDtypeStruct(particles.shape, F32),
            ),
            in_specs=[hbm] * 9,
            out_specs=(vmem, vmem),
            scratch_shapes=[
                pltpu.VMEM(fields.shape, F32),
                pltpu.VMEM(pore.shape, I32),
                pltpu.VMEM(rate.shape, F32),
                pltpu.VMEM(particles.shape, F32),
                pltpu.VMEM(occupancy.shape, I32),
                pltpu.VMEM(slot_cell.shape, I32),
                pltpu.VMEM(send_slot.shape, I32),
                pltpu.SMEM((STEPS * 8,), I32),
                pltpu.VMEM(land_slot.shape, I32),
                pltpu.SemaphoreType.DMA((11,)),
                pltpu.VMEM((8, SLOTS, BLOCKS), F32),
                pltpu.VMEM((4, BLOCKS, SLOTS), F32),
                pltpu.VMEM((SLOTS, BLOCKS), F32),
                pltpu.VMEM((SLOTS, BLOCKS), F32),
                pltpu.VMEM((13 * LIVE, 2 * BLOCKS), BF16),
                pltpu.VMEM((4, BLOCKS, SLOTS), F32),
                pltpu.VMEM((CX, FLAT, SLOTS), BF16),
                pltpu.VMEM((STEPS, 4, CX, FLAT), F32),
                pltpu.VMEM((STEPS, 2, 2, 8, FLAT), F32),
                pltpu.VMEM((STEPS, 2, 2, CX, 128), F32),
                pltpu.VMEM((STEPS, 2, 2, 8, FLAT), F32),
                pltpu.VMEM((STEPS, 2, 2, CX, 128), F32),
                pltpu.VMEM((4, 4, 4, CAP), F32),
                pltpu.VMEM((4, 4, 4, CAP), F32),
                pltpu.VMEM((4, 4, 128), F32),
                pltpu.VMEM((4, 4, 4, 128), F32),
                pltpu.SemaphoreType.DMA((copies,)),
                pltpu.SemaphoreType.DMA((copies,)),
            ],
            compiler_params=pltpu.CompilerParams(
                collective_id=0, has_side_effects=True, vmem_limit_bytes=48 << 20
            ),
        )(
            *[
                pltpu.with_memory_space_constraint(x, pltpu.HBM)
                for x in (
                    fields,
                    pore,
                    rate,
                    particles,
                    occupancy,
                    slot_cell,
                    send_slot,
                    send_count.reshape(STEPS * 8),
                    land_slot,
                )
            ]
        )

        def store(a, b, a_out, b_out, sem):
            both = [
                pltpu.make_async_copy(b, b_out, sem.at[0]),
                pltpu.make_async_copy(a, a_out, sem.at[1]),
            ]
            for copy in both:
                copy.start()
            for copy in both:
                copy.wait()

        return pl.pallas_call(
            store,
            out_shape=(
                jax.ShapeDtypeStruct(fields.shape, F32),
                jax.ShapeDtypeStruct(particles.shape, F32),
            ),
            in_specs=[vmem] * 2,
            out_specs=(hbm, hbm),
            scratch_shapes=[pltpu.SemaphoreType.DMA((2,))],
            compiler_params=pltpu.CompilerParams(vmem_limit_bytes=4 << 20),
        )(*results)

    return jax.shard_map(
        body,
        mesh=mesh,
        in_specs=(
            P(None, "gx", "gy"),
            P("gx", "gy"),
            P("gx", "gy"),
            P(None, "gx", "gy"),
            P("gx", "gy"),
            P("gx", "gy"),
            P(None, "gx", "gy"),
            P(None, "gx", "gy"),
            P(None, "gx", "gy"),
        ),
        out_specs=(P(None, "gx", "gy"), P(None, "gx", "gy")),
        check_vma=False,
    )
```

```python
import jax
import jax.numpy as jnp
from jax import lax
from jax.experimental import pallas as pl
from jax.experimental.pallas import tpu as pltpu
from jax.sharding import PartitionSpec as P

CX = 16
CY = 16
CZ = 16
SLOTS = 128
STEPS = 2
CAP = 384
DIAG = 16
BLOCKS = CX * CY
FLAT = CY * CZ
AXIAL = 4 * CAP
LIST = AXIAL + 128
LIVE = 96
DEAD = 32
SPAN = SLOTS - DEAD
COURANT = 0.25
ROT = 4.0
MOVES = ((1, 0), (-1, 0), (0, 1), (0, -1), (1, 1), (1, -1), (-1, 1), (-1, -1))
F32 = jnp.float32
BF16 = jnp.bfloat16
I32 = jnp.int32
MESH = pl.DeviceIdType.MESH


def iota(shape, dim):
    return lax.broadcasted_iota(I32, shape, dim)


def split(x):
    high = (x * 0.995).astype(BF16)
    low = (x - high.astype(F32)).astype(BF16)
    return high, low


def dot(a, b):
    return lax.dot_general(a, b, (((1,), (0,)), ((), ())), preferred_element_type=F32)


def dot_nt(a, b):
    return lax.dot_general(a, b, (((1,), (1,)), ((), ())), preferred_element_type=F32)


def roll(x, by, axis):
    return pltpu.roll(x, by % x.shape[axis], axis)


def onehot_rows(row, size):
    n = row.shape[1]
    return jnp.where(iota((size, n), 0) == row, 1.0, 0.0).astype(BF16)


def block_row(slot):
    block = slot >> 7
    return (block & 15) * CX + (block >> 4)


def flux_of(comps, coef, axis_n, move):
    nxt = [move(w, 1) for w in comps]

    def centred(w, w_next):
        return 7.0 / 12.0 * (w + w_next) - 1.0 / 12.0 * (move(w, -1) + move(w, 2))

    out = []
    for c in range(4):
        value = -0.5 * (nxt[c] - comps[c])
        if c == 0:
            value = value + centred(comps[1 + axis_n], nxt[1 + axis_n])
        if c == 1 + axis_n:
            value = value + centred(comps[0], nxt[0])
        out.append(coef * value)
    return out


def kernel(
    nx,
    ny,
    fields_hbm,
    pore_hbm,
    rate_hbm,
    part_hbm,
    occ_hbm,
    cell_hbm,
    send_hbm,
    count_hbm,
    land_hbm,
    fields_out,
    part_out,
    fields_ref,
    pore_ref,
    rate_ref,
    part_ref,
    occ_ref,
    cell_ref,
    send_ref,
    count_ref,
    land_ref,
    load_sem,
    state,
    natural,
    keep_turned,
    relax_turned,
    split_state,
    values,
    deposit_hot,
    total,
    hx_out,
    hy_out,
    hx,
    hy,
    axial_out,
    axial_in,
    diag_out,
    diag_in,
    send_sem,
    recv_sem,
):
    ix = lax.axis_index("gx")
    iy = lax.axis_index("gy")

    def device(move):
        return (lax.rem(ix + move[0] + nx, nx), lax.rem(iy + move[1] + ny, ny))

    def present(move):
        x, y = ix - move[0], iy - move[1]
        return (x >= 0) & (x < nx) & (y >= 0) & (y < ny)

    loads = []
    for src, dst in (
        (rate_hbm, rate_ref),
        (cell_hbm, cell_ref),
        (part_hbm.at[3:7], part_ref.at[3:7]),
        (occ_hbm, occ_ref),
        (send_hbm, send_ref),
        (count_hbm, count_ref),
        (part_hbm.at[0:3], part_ref.at[0:3]),
        (part_hbm.at[7:8], part_ref.at[7:8]),
        (pore_hbm, pore_ref),
        (fields_hbm, fields_ref),
        (land_hbm, land_ref),
    ):
        copy = pltpu.make_async_copy(src, dst, load_sem.at[len(loads)])
        copy.start()
        loads.append(copy)

    copies = []

    def send(src, dst, move):
        k = len(copies)
        copy = pltpu.make_async_remote_copy(
            src_ref=src,
            dst_ref=dst,
            send_sem=send_sem.at[k],
            recv_sem=recv_sem.at[k],
            device_id=device(move),
            device_id_type=MESH,
        )
        copy.start()
        copies.append(copy)
        return copy

    barrier = pltpu.get_barrier_semaphore()
    for move in MOVES:
        pl.semaphore_signal(barrier, inc=1, device_id=device(move), device_id_type=MESH)

    def lanes_of(y):
        return slice(y * SLOTS, (y + 1) * SLOTS)

    def rows_of(y):
        return slice(y * CX, (y + 1) * CX)

    loads[0].wait()
    loads[1].wait()
    rate = rate_ref[...]
    keep = jnp.exp(-rate)
    relax = jnp.exp(-rate / ROT)
    lane = iota((CX, SLOTS), 1)

    keep_slot, relax_slot = [], []
    for y in range(CY):
        half = slice((y // 8) * 128, (y // 8) * 128 + 128)
        index = cell_ref[:, lanes_of(y)] + (y % 8) * CZ
        keep_slot.append(jnp.take_along_axis(keep[:, half], index, axis=1))
        relax_slot.append(jnp.take_along_axis(relax[:, half], index, axis=1))

    for copy in loads[2:6]:
        copy.wait()
    occ = occ_ref[...]
    live = [lane < occ[:, y : y + 1] for y in range(CY)]

    def turn(pieces):
        return jnp.transpose(jnp.concatenate(pieces, axis=0))

    def load_state(c):
        pieces = [jnp.where(live[y], part_ref[c, :, lanes_of(y)], 0.0) for y in range(CY)]
        if c >= 3 and c < 7:
            for y in range(CY):
                natural[c - 3, rows_of(y), :] = pieces[y]
        state[c] = turn(pieces)

    def put_split(k, value):
        high, low = split(value[:LIVE])
        rows = slice(k * LIVE, (k + 1) * LIVE)
        split_state[rows, 0:BLOCKS] = high
        split_state[rows, BLOCKS : 2 * BLOCKS] = low

    def diag_rows(ref, step):
        at = iota((8, 128), 1) // DIAG
        out = jnp.zeros((8, 128), I32)
        for d in range(4):
            row = jnp.broadcast_to(ref[step * 8 + 4 + d][:, 0:128], (8, 128))
            out = jnp.where(at == d, roll(row, d * DIAG, 1), out)
        return out[0:1]

    def slots_of(ref, step):
        slots = [ref[step * 8 + d] for d in range(4)] + [diag_rows(ref, step)]
        return jnp.concatenate(slots, axis=1)

    def send_list(step):
        slots = slots_of(send_ref, step)
        used = [
            (iota((1, CAP), 1) < count_ref[step * 8 + d]).astype(I32) for d in range(4)
        ]
        at = iota((1, 128), 1)
        ok = at < 0
        for d in range(4):
            ok = ok | ((at >= d * DIAG) & (at < d * DIAG + count_ref[step * 8 + 4 + d]))
        used.append(ok.astype(I32))
        row = jnp.where(jnp.concatenate(used, axis=1) > 0, block_row(slots), -1)
        flag = jnp.broadcast_to(used[4].astype(F32), (8, 128))
        return row, slots & 127, onehot_rows(row, BLOCKS), flag

    def gather(listed, first, parts, starts):
        _, place, row_hot, _ = listed
        count = 4 * len(parts)
        for start in starts:
            stop = min(start + 256, LIST)
            n = stop - start
            hot = row_hot[:, start:stop]
            mine = iota((LIVE, n), 0) == place[:, start:stop]
            product = dot(
                split_state[first * LIVE : (first + count) * LIVE, :],
                jnp.concatenate([hot, hot], axis=0),
            )
            got = [
                jnp.sum(
                    jnp.where(mine, product[c * LIVE : (c + 1) * LIVE], 0.0),
                    axis=0,
                    keepdims=True,
                )
                for c in range(count)
            ]
            for i, part in enumerate(parts):
                four = jnp.concatenate(got[4 * i : 4 * i + 4], axis=0)
                for tile in range(start // 128, stop // 128):
                    piece = four[:, tile * 128 - start : tile * 128 - start + 128]
                    if tile < AXIAL // 128:
                        at = (tile % 3) * 128
                        axial_out[tile // 3, part, :, at : at + 128] = piece
                    else:
                        diag_out[part] = piece

    def send_axial(first, count):
        parts = pl.ds(first, count)
        return [send(axial_out.at[d, parts], axial_in.at[d, parts], MOVES[d]) for d in (2, 3, 0, 1)]

    def send_corners(first, count):
        parts = pl.ds(first, count)
        return [
            send(diag_out.at[parts], diag_in.at[d, parts], MOVES[4 + d]) for d in range(4)
        ]

    def deposit(weight):
        for y in range(CY):
            w = weight(y)
            values[0, rows_of(y), :] = w
            for c in range(3):
                values[1 + c, rows_of(y), :] = w * natural[c, rows_of(y), :]
        own = iota((CY, FLAT), 1) // CZ == iota((CY, FLAT), 0)
        out = [[] for _ in range(4)]
        for x in range(CX):
            picked = jnp.concatenate(
                [values[c, pl.ds(x, CY, stride=CX), :] for c in range(4)], axis=0
            )
            high, low = split(picked)
            both = dot_nt(jnp.concatenate([high, low], axis=0), deposit_hot[x])
            both = both[: 4 * CY] + both[4 * CY :]
            for c in range(4):
                part = jnp.where(own, both[c * CY : (c + 1) * CY], 0.0)
                out[c].append(jnp.sum(part, axis=0, keepdims=True))
        return [jnp.concatenate(o, axis=0) for o in out]

    def pack_x(parts, shift):
        at = iota((8, FLAT), 0) // 2
        out = jnp.zeros((8, FLAT), F32)
        for i, part in enumerate(parts):
            out = jnp.where(at == i, roll(part, 2 * i - shift, 0), out)
        return out

    def pack_y(parts, shift):
        at = iota((CX, 128), 1) // 32
        out = jnp.zeros((CX, 128), F32)
        for i, part in enumerate(parts):
            out = jnp.where(at == i, roll(part, 32 * i - shift, 1), out)
        return out

    def send_halo(step):
        own = [total[step, c] for c in range(4)]
        hx_out[step, 0, 0] = pack_x([w[8:16] for w in own], 6)
        hx_out[step, 1, 0] = pack_x([w[0:8] for w in own], 0)
        hy_out[step, 0, 0] = pack_y([w[:, 128:256] for w in own], 96)
        hy_out[step, 1, 0] = pack_y([w[:, 0:128] for w in own], 0)
        if step == 0:
            for d in range(4):
                counts = [count_ref[s * 8 + d].astype(F32) for s in range(STEPS)]
                if d < 2:
                    rows = slice(8, 16) if d == 0 else slice(0, 8)
                    packed = pack_x([fluid[rows], keep[rows]], 6 if d == 0 else 0)
                    at = iota((8, FLAT), 0)
                    packed = jnp.where(at == 4, counts[0], jnp.where(at == 5, counts[1], packed))
                    hx_out[0, d, 1] = packed
                else:
                    lanes = slice(128, 256) if d == 2 else slice(0, 128)
                    packed = pack_y([fluid[:, lanes], keep[:, lanes]], 96 if d == 2 else 0)
                    at = iota((CX, 128), 1) // 32
                    packed = jnp.where(at == 2, counts[0], jnp.where(at == 3, counts[1], packed))
                    hy_out[0, d - 2, 1] = packed
            return [
                send(hy_out.at[0, 0], hy.at[0, 0], MOVES[2]),
                send(hy_out.at[0, 1], hy.at[0, 1], MOVES[3]),
                send(hx_out.at[0, 0], hx.at[0, 0], MOVES[0]),
                send(hx_out.at[0, 1], hx.at[0, 1], MOVES[1]),
            ]
        return [
            send(hy_out.at[step, 0, 0], hy.at[step, 0, 0], MOVES[2]),
            send(hy_out.at[step, 1, 0], hy.at[step, 1, 0], MOVES[3]),
            send(hx_out.at[step, 0, 0], hx.at[step, 0, 0], MOVES[0]),
            send(hx_out.at[step, 1, 0], hx.at[step, 1, 0], MOVES[1]),
        ]

    def ring_x(own, low, high, i):
        at = iota((8, FLAT), 0)
        low = jnp.where((at >= 6) & present(MOVES[0]), roll(low, 6 - 2 * i, 0), 0.0)
        edge = jnp.where((at < 2) & present(MOVES[1]), roll(high, -2 * i, 0), low)
        return jnp.concatenate([own, edge], axis=0)

    def ring_y(own, low, high, i):
        at = iota((CX, 128), 1)
        low = jnp.where((at >= 96) & present(MOVES[2]), roll(low, 96 - 32 * i, 1), 0.0)
        edge = jnp.where((at < 32) & present(MOVES[3]), roll(high, -32 * i, 1), low)
        return jnp.concatenate([own, edge], axis=1)

    def move_x(w, k):
        return roll(w, -k, 0)

    def move_y(w, k):
        return roll(w, -k * CZ, 1)

    zpos = iota((CX, FLAT), 1) % CZ

    def move_z(w, k):
        inside = (zpos + k >= 0) & (zpos + k < CZ)
        return jnp.where(inside, roll(w, -k, 1), 0.0)

    def coefs():
        def one(f, k, move):
            return f * move(f, 1) * (1.0 - 0.5 * (k + move(k, 1)))

        ex = [(hx[0, 0, 1], hx[0, 1, 1], i) for i in range(2)]
        ey = [(hy[0, 0, 1], hy[0, 1, 1], i) for i in range(2)]
        x = one(ring_x(fluid, *ex[0]), ring_x(keep, *ex[1]), move_x)
        y = one(ring_y(fluid, *ey[0]), ring_y(keep, *ey[1]), move_y)
        return x, y, one(fluid, keep, move_z)

    def divergence(step, coef):
        own = [total[step, c] for c in range(4)]
        xs = [ring_x(own[c], hx[step, 0, 0], hx[step, 1, 0], c) for c in range(4)]
        ys = [ring_y(own[c], hy[step, 0, 0], hy[step, 1, 0], c) for c in range(4)]
        fx = flux_of(xs, coef[0], 0, move_x)
        fy = flux_of(ys, coef[1], 1, move_y)
        fz = flux_of(own, coef[2], 2, move_z)
        out = []
        for c in range(4):
            dx = (fx[c] - move_x(fx[c], -1))[:CX]
            dy = (fy[c] - move_y(fy[c], -1))[:, :FLAT]
            out.append(dx + dy + (fz[c] - move_z(fz[c], -1)))
        return out

    def collide(c, value):
        if c < 3:
            return value + COURANT * state[3 + c]
        if c == 6:
            return value * keep_turned[...]
        return 1.0 + (value - 1.0) * relax_turned[...]

    def fit_list(step):
        at = iota((1, CAP), 1).astype(F32)
        fits = []
        for d in range(4):
            if d < 2:
                count = hx[0, d, 1][4 + step : 5 + step, 0:1]
            else:
                count = hy[0, d - 2, 1][0:1, 64 + 32 * step : 65 + 32 * step]
            fits.append((at < jnp.broadcast_to(count, (1, CAP))) & present(MOVES[d]))
        lane = iota((4, 128), 1)
        got = jnp.zeros((4, 128), F32)
        for d in range(4):
            mine = (lane % 64) // DIAG == d
            got = jnp.where(mine & present(MOVES[4 + d]), diag_in[d, 0], got)
        flag = (roll(got, 64, 1) > 0.5) & (lane < 64)
        fits.append(flag[2 * step : 2 * step + 1])
        return jnp.concatenate([f.astype(F32) for f in fits], axis=1) > 0.5

    def arrived(fit, rows):
        lane = iota((4, 128), 1)
        corners = {}
        for part in sorted({part for part, _ in rows}):
            got = jnp.zeros((4, 128), F32)
            for d in range(4):
                mine = (lane % 64) // DIAG == d
                got = jnp.where(mine & present(MOVES[4 + d]), diag_in[d, part], got)
            corners[part] = got
        out = []
        for part, at in rows:
            pieces = [axial_in[d, part, at : at + 1, :] for d in range(4)]
            pieces.append(corners[part][at : at + 1])
            out.append(jnp.where(fit, jnp.concatenate(pieces, axis=1), 0.0))
        return out

    keep_turned[...] = turn(keep_slot)
    for c in (6, 3, 4, 5):
        load_state(c)
    weight = collide(6, state[6])
    state[6] = weight
    put_split(0, weight)
    for c in range(3):
        put_split(1 + c, state[3 + c])
    listed = [send_list(step) for step in range(STEPS)]
    axial_starts = list(range(0, AXIAL, 256))
    gather(listed[0], 0, [0], axial_starts + [AXIAL])
    flags = jnp.where(iota((8, 128), 0) < 2, listed[0][3], listed[1][3])
    flags = roll(flags, 64, 1)[0:4]
    diag_out[0] = jnp.where(iota((4, 128), 1) < 64, diag_out[0], flags)

    for x in range(CX):
        for y in range(CY):
            mine = iota((CZ, SLOTS), 0) == jnp.broadcast_to(
                cell_ref[x : x + 1, lanes_of(y)], (CZ, SLOTS)
            )
            deposit_hot[x, y * CZ : (y + 1) * CZ, :] = jnp.where(mine, 1.0, 0.0).astype(BF16)
    moments = deposit(lambda y: natural[3, rows_of(y), :])
    for copy in loads[8:]:
        copy.wait()
    fluid = pore_ref[...].astype(F32)
    for c in range(4):
        total[0, c] = (fields_ref[c] + moments[c]) * fluid
    pl.semaphore_wait(barrier, len(MOVES))
    first = send_corners(0, 1) + send_axial(0, 1)
    halo = send_halo(0)

    for copy in loads[6:8]:
        copy.wait()
    relax_turned[...] = turn(relax_slot)
    for k, c in enumerate((0, 1, 2, 7)):
        load_state(c)
        value = collide(c, state[c])
        put_split(9 + k, value)
        value = collide(c, value)
        put_split(5 + k, value)
        state[c] = value
    weight = collide(6, state[6])
    put_split(4, weight)
    state[6] = weight
    gather(listed[0], 9, [1], axial_starts + [AXIAL])
    gather(listed[1], 1, [2, 3], axial_starts + [AXIAL])
    late = send_corners(1, 3) + send_axial(1, 3)

    left = [
        dot_nt(onehot_rows(place, LIVE), row_hot) > 0.5 for _, place, row_hot, _ in listed
    ]
    gone = jnp.transpose(
        jnp.concatenate(
            [left[0].astype(F32), jnp.zeros((SLOTS - LIVE, BLOCKS), F32)], axis=0
        )
    )
    stay = deposit(
        lambda y: jnp.where(
            gone[rows_of(y)] > 0.5, 0.0, natural[3, rows_of(y), :] * keep_slot[y]
        )
    )
    slots = [slots_of(land_ref, step) for step in range(STEPS)]
    place_hots = [onehot_rows((t & 127) - DEAD, SPAN) for t in slots]
    row = block_row(slots[0])
    row_hots = [onehot_rows(block_row(t), BLOCKS) for t in slots]
    cell_all = turn([cell_ref[:, lanes_of(y)].astype(F32) for y in range(CY)])
    found = dot(cell_all[DEAD:].astype(BF16), row_hots[0])
    z = jnp.sum(
        jnp.where(iota((SPAN, LIST), 0) == (slots[0] & 127) - DEAD, found, 0.0),
        axis=0,
        keepdims=True,
    )
    flat_cell = (row >> 4).astype(F32) * CZ + z
    cell_hot = jnp.where(
        iota((FLAT, LIST), 0).astype(F32) == flat_cell, 1.0, 0.0
    ).astype(BF16)
    x_mine = iota((CX, LIST), 0) == (row & 15)
    table = jnp.concatenate([*split(keep), *split(relax)], axis=0)
    factors = dot(table, cell_hot)

    def factor(k):
        both = factors[2 * k * CX : (2 * k + 1) * CX] + factors[(2 * k + 1) * CX : (2 * k + 2) * CX]
        return jnp.sum(jnp.where(x_mine, both, 0.0), axis=0, keepdims=True)

    keep_land, relax_land = factor(0), factor(1)

    for copy in first + halo:
        copy.wait()
    fit = [fit_list(step) for step in range(STEPS)]
    w, vx, vy, vz = arrived(fit[0], [(0, k) for k in range(4)])
    highs, lows = [], []
    for value in (w, w * vx, w * vy, w * vz):
        high, low = split(jnp.where(x_mine, value, 0.0))
        highs.append(high)
        lows.append(low)
    landed = dot_nt(jnp.concatenate(highs + lows, axis=0), cell_hot)
    landed = landed[: 4 * CX] + landed[4 * CX :]
    coef = coefs()
    div = divergence(0, coef)
    fields = [
        fields_ref[c] - COURANT * div[c] + (1.0 - keep) * moments[c] for c in range(4)
    ]
    moments = [stay[c] + landed[c * CX : (c + 1) * CX] for c in range(4)]
    for c in range(4):
        total[1, c] = (fields[c] + moments[c]) * fluid
    halo = send_halo(1)

    for c in range(8):
        rest = 1.0 - relax_turned[:LIVE] if c == 7 else 0.0
        value = jnp.where(left[0], rest, state[c, :LIVE])
        state[c, :LIVE] = jnp.where(left[1], 0.0, value)

    def land(step, comps, news):
        parts = []
        for new in news:
            high, low = split(new)
            parts += [place_hots[step] * high, place_hots[step] * low]
        if 7 in comps:
            parts.append(place_hots[step] * fit[step].astype(F32).astype(BF16))
        got = dot_nt(jnp.concatenate(parts, axis=0), row_hots[step])
        for i, c in enumerate(comps):
            new = got[2 * i * SPAN : (2 * i + 1) * SPAN]
            new = new + got[(2 * i + 1) * SPAN : (2 * i + 2) * SPAN]
            before = state[c, DEAD:]
            if c == 7:
                before = jnp.where(got[2 * len(comps) * SPAN :] > 0.5, 0.0, before)
            state[c, DEAD:] = before + new

    land(0, (6, 3, 4, 5), (w * keep_land, vx, vy, vz))
    for copy in late:
        copy.wait()
    px, py, pz, rot = arrived(fit[0], [(1, k) for k in range(4)])
    land(
        0,
        (0, 1, 2, 7),
        (
            px + COURANT * vx,
            py + COURANT * vy,
            pz + COURANT * vz,
            jnp.where(fit[0], 1.0 + (rot - 1.0) * relax_land, 0.0),
        ),
    )
    land(
        1,
        (3, 4, 5, 6, 0, 1, 2, 7),
        arrived(fit[1], [(part, k) for part in (2, 3) for k in range(4)]),
    )
    for c in range(8):
        whole = jnp.transpose(state[c])
        for y in range(CY):
            part_out[c, :, lanes_of(y)] = whole[rows_of(y)]
    for copy in halo:
        copy.wait()
    div = divergence(1, coef)
    for c in range(4):
        fields_out[c] = fields[c] - COURANT * div[c] + (1.0 - keep) * moments[c]


def solution(mesh):
    nx, ny = mesh.shape["gx"], mesh.shape["gy"]

    def body(fields, pore, rate, particles, occupancy, slot_cell, send_slot, send_count, land_slot):
        vmem = pl.BlockSpec(memory_space=pltpu.VMEM)
        hbm = pl.BlockSpec(memory_space=pltpu.HBM)
        copies = 8 * STEPS + 8 + 4 * STEPS

        def run(*refs):
            kernel(nx, ny, *refs)

        results = pl.pallas_call(
            run,
            out_shape=(
                jax.ShapeDtypeStruct(fields.shape, F32),
                jax.ShapeDtypeStruct(particles.shape, F32),
            ),
            in_specs=[hbm] * 9,
            out_specs=(vmem, vmem),
            scratch_shapes=[
                pltpu.VMEM(fields.shape, F32),
                pltpu.VMEM(pore.shape, I32),
                pltpu.VMEM(rate.shape, F32),
                pltpu.VMEM(particles.shape, F32),
                pltpu.VMEM(occupancy.shape, I32),
                pltpu.VMEM(slot_cell.shape, I32),
                pltpu.VMEM(send_slot.shape, I32),
                pltpu.SMEM((STEPS * 8,), I32),
                pltpu.VMEM(land_slot.shape, I32),
                pltpu.SemaphoreType.DMA((11,)),
                pltpu.VMEM((8, SLOTS, BLOCKS), F32),
                pltpu.VMEM((4, BLOCKS, SLOTS), F32),
                pltpu.VMEM((SLOTS, BLOCKS), F32),
                pltpu.VMEM((SLOTS, BLOCKS), F32),
                pltpu.VMEM((13 * LIVE, 2 * BLOCKS), BF16),
                pltpu.VMEM((4, BLOCKS, SLOTS), F32),
                pltpu.VMEM((CX, FLAT, SLOTS), BF16),
                pltpu.VMEM((STEPS, 4, CX, FLAT), F32),
                pltpu.VMEM((STEPS, 2, 2, 8, FLAT), F32),
                pltpu.VMEM((STEPS, 2, 2, CX, 128), F32),
                pltpu.VMEM((STEPS, 2, 2, 8, FLAT), F32),
                pltpu.VMEM((STEPS, 2, 2, CX, 128), F32),
                pltpu.VMEM((4, 4, 4, CAP), F32),
                pltpu.VMEM((4, 4, 4, CAP), F32),
                pltpu.VMEM((4, 4, 128), F32),
                pltpu.VMEM((4, 4, 4, 128), F32),
                pltpu.SemaphoreType.DMA((copies,)),
                pltpu.SemaphoreType.DMA((copies,)),
            ],
            compiler_params=pltpu.CompilerParams(
                collective_id=0, has_side_effects=True, vmem_limit_bytes=48 << 20
            ),
        )(
            *[
                pltpu.with_memory_space_constraint(x, pltpu.HBM)
                for x in (
                    fields,
                    pore,
                    rate,
                    particles,
                    occupancy,
                    slot_cell,
                    send_slot,
                    send_count.reshape(STEPS * 8),
                    land_slot,
                )
            ]
        )

        def store(a, b, a_out, b_out, sem):
            both = [
                pltpu.make_async_copy(b, b_out, sem.at[0]),
                pltpu.make_async_copy(a, a_out, sem.at[1]),
            ]
            for copy in both:
                copy.start()
            for copy in both:
                copy.wait()

        return pl.pallas_call(
            store,
            out_shape=(
                jax.ShapeDtypeStruct(fields.shape, F32),
                jax.ShapeDtypeStruct(particles.shape, F32),
            ),
            in_specs=[vmem] * 2,
            out_specs=(hbm, hbm),
            scratch_shapes=[pltpu.SemaphoreType.DMA((2,))],
            compiler_params=pltpu.CompilerParams(vmem_limit_bytes=4 << 20),
        )(*results)

    return jax.shard_map(
        body,
        mesh=mesh,
        in_specs=(
            P(None, "gx", "gy"),
            P("gx", "gy"),
            P("gx", "gy"),
            P(None, "gx", "gy"),
            P("gx", "gy"),
            P("gx", "gy"),
            P(None, "gx", "gy"),
            P(None, "gx", "gy"),
            P(None, "gx", "gy"),
        ),
        out_specs=(P(None, "gx", "gy"), P(None, "gx", "gy")),
        check_vma=False,
    )
```

```python
import jax
import jax.numpy as jnp
from jax import lax
from jax.experimental import pallas as pl
from jax.experimental.pallas import tpu as pltpu
from jax.sharding import PartitionSpec as P

CX = 16
CY = 16
CZ = 16
SLOTS = 128
STEPS = 2
CAP = 384
DIAG = 16
BLOCKS = CX * CY
FLAT = CY * CZ
AXIAL = 4 * CAP
LIST = AXIAL + 128
LIVE = 96
DEAD = 32
SPAN = SLOTS - DEAD
COURANT = 0.25
ROT = 4.0
MOVES = ((1, 0), (-1, 0), (0, 1), (0, -1), (1, 1), (1, -1), (-1, 1), (-1, -1))
F32 = jnp.float32
BF16 = jnp.bfloat16
I32 = jnp.int32
MESH = pl.DeviceIdType.MESH


def iota(shape, dim):
    return lax.broadcasted_iota(I32, shape, dim)


def split(x):
    high = (x * 0.995).astype(BF16)
    low = (x - high.astype(F32)).astype(BF16)
    return high, low


def dot(a, b):
    return lax.dot_general(a, b, (((1,), (0,)), ((), ())), preferred_element_type=F32)


def dot_nt(a, b):
    return lax.dot_general(a, b, (((1,), (1,)), ((), ())), preferred_element_type=F32)


def roll(x, by, axis):
    return pltpu.roll(x, by % x.shape[axis], axis)


def onehot_rows(row, size):
    n = row.shape[1]
    return jnp.where(iota((size, n), 0) == row, 1.0, 0.0).astype(BF16)


def block_row(slot):
    block = slot >> 7
    return (block & 15) * CX + (block >> 4)


def flux_of(comps, coef, axis_n, move):
    nxt = [move(w, 1) for w in comps]

    def centred(w, w_next):
        return 7.0 / 12.0 * (w + w_next) - 1.0 / 12.0 * (move(w, -1) + move(w, 2))

    out = []
    for c in range(4):
        value = -0.5 * (nxt[c] - comps[c])
        if c == 0:
            value = value + centred(comps[1 + axis_n], nxt[1 + axis_n])
        if c == 1 + axis_n:
            value = value + centred(comps[0], nxt[0])
        out.append(coef * value)
    return out


def kernel(
    nx,
    ny,
    fields_hbm,
    pore_hbm,
    rate_hbm,
    part_hbm,
    occ_hbm,
    cell_hbm,
    send_hbm,
    count_hbm,
    land_hbm,
    fields_out,
    part_out,
    fields_ref,
    pore_ref,
    rate_ref,
    part_ref,
    occ_ref,
    cell_ref,
    send_ref,
    count_ref,
    land_ref,
    load_sem,
    state,
    natural,
    keep_turned,
    relax_turned,
    split_state,
    values,
    deposit_hot,
    total,
    hx_out,
    hy_out,
    hx,
    hy,
    axial_out,
    axial_in,
    diag_out,
    diag_in,
    send_sem,
    recv_sem,
):
    ix = lax.axis_index("gx")
    iy = lax.axis_index("gy")

    def device(move):
        return (lax.rem(ix + move[0] + nx, nx), lax.rem(iy + move[1] + ny, ny))

    def present(move):
        x, y = ix - move[0], iy - move[1]
        return (x >= 0) & (x < nx) & (y >= 0) & (y < ny)

    loads = []
    for src, dst in (
        (rate_hbm, rate_ref),
        (cell_hbm, cell_ref),
        (part_hbm.at[3:7], part_ref.at[3:7]),
        (occ_hbm, occ_ref),
        (send_hbm, send_ref),
        (count_hbm, count_ref),
        (part_hbm.at[0:3], part_ref.at[0:3]),
        (part_hbm.at[7:8], part_ref.at[7:8]),
        (pore_hbm, pore_ref),
        (fields_hbm, fields_ref),
        (land_hbm, land_ref),
    ):
        copy = pltpu.make_async_copy(src, dst, load_sem.at[len(loads)])
        copy.start()
        loads.append(copy)

    copies = []

    def send(src, dst, move):
        k = len(copies)
        copy = pltpu.make_async_remote_copy(
            src_ref=src,
            dst_ref=dst,
            send_sem=send_sem.at[k],
            recv_sem=recv_sem.at[k],
            device_id=device(move),
            device_id_type=MESH,
        )
        copy.start()
        copies.append(copy)
        return copy

    barrier = pltpu.get_barrier_semaphore()
    for move in MOVES:
        pl.semaphore_signal(barrier, inc=1, device_id=device(move), device_id_type=MESH)

    def lanes_of(y):
        return slice(y * SLOTS, (y + 1) * SLOTS)

    def rows_of(y):
        return slice(y * CX, (y + 1) * CX)

    loads[0].wait()
    loads[1].wait()
    rate = rate_ref[...]
    keep = jnp.exp(-rate)
    relax = jnp.exp(-rate / ROT)
    lane = iota((CX, SLOTS), 1)

    keep_slot, relax_slot = [], []
    for y in range(CY):
        half = slice((y // 8) * 128, (y // 8) * 128 + 128)
        index = cell_ref[:, lanes_of(y)] + (y % 8) * CZ
        keep_slot.append(jnp.take_along_axis(keep[:, half], index, axis=1))
        relax_slot.append(jnp.take_along_axis(relax[:, half], index, axis=1))

    for copy in loads[2:6]:
        copy.wait()
    occ = occ_ref[...]
    live = [lane < occ[:, y : y + 1] for y in range(CY)]

    def turn(pieces):
        return jnp.transpose(jnp.concatenate(pieces, axis=0))

    def load_state(c):
        pieces = [jnp.where(live[y], part_ref[c, :, lanes_of(y)], 0.0) for y in range(CY)]
        if c >= 3 and c < 7:
            for y in range(CY):
                natural[c - 3, rows_of(y), :] = pieces[y]
        state[c] = turn(pieces)

    def put_split(k, value):
        high, low = split(value[:LIVE])
        rows = slice(k * LIVE, (k + 1) * LIVE)
        split_state[rows, 0:BLOCKS] = high
        split_state[rows, BLOCKS : 2 * BLOCKS] = low

    def diag_rows(ref, step):
        at = iota((8, 128), 1) // DIAG
        out = jnp.zeros((8, 128), I32)
        for d in range(4):
            row = jnp.broadcast_to(ref[step * 8 + 4 + d][:, 0:128], (8, 128))
            out = jnp.where(at == d, roll(row, d * DIAG, 1), out)
        return out[0:1]

    def slots_of(ref, step):
        slots = [ref[step * 8 + d] for d in range(4)] + [diag_rows(ref, step)]
        return jnp.concatenate(slots, axis=1)

    def send_list(step):
        slots = slots_of(send_ref, step)
        used = [
            (iota((1, CAP), 1) < count_ref[step * 8 + d]).astype(I32) for d in range(4)
        ]
        at = iota((1, 128), 1)
        ok = at < 0
        for d in range(4):
            ok = ok | ((at >= d * DIAG) & (at < d * DIAG + count_ref[step * 8 + 4 + d]))
        used.append(ok.astype(I32))
        row = jnp.where(jnp.concatenate(used, axis=1) > 0, block_row(slots), -1)
        flag = jnp.broadcast_to(used[4].astype(F32), (8, 128))
        return row, slots & 127, onehot_rows(row, BLOCKS), flag

    def gather(listed, first, parts, starts):
        _, place, row_hot, _ = listed
        count = 4 * len(parts)
        for start in starts:
            stop = min(start + 256, LIST)
            n = stop - start
            hot = row_hot[:, start:stop]
            mine = iota((LIVE, n), 0) == place[:, start:stop]
            product = dot(
                split_state[first * LIVE : (first + count) * LIVE, :],
                jnp.concatenate([hot, hot], axis=0),
            )
            got = [
                jnp.sum(
                    jnp.where(mine, product[c * LIVE : (c + 1) * LIVE], 0.0),
                    axis=0,
                    keepdims=True,
                )
                for c in range(count)
            ]
            for i, part in enumerate(parts):
                four = jnp.concatenate(got[4 * i : 4 * i + 4], axis=0)
                for tile in range(start // 128, stop // 128):
                    piece = four[:, tile * 128 - start : tile * 128 - start + 128]
                    if tile < AXIAL // 128:
                        at = (tile % 3) * 128
                        axial_out[tile // 3, part, :, at : at + 128] = piece
                    else:
                        diag_out[part] = piece

    def send_axial(first, count):
        parts = pl.ds(first, count)
        return [send(axial_out.at[d, parts], axial_in.at[d, parts], MOVES[d]) for d in (2, 3, 0, 1)]

    def send_corners(first, count):
        parts = pl.ds(first, count)
        return [
            send(diag_out.at[parts], diag_in.at[d, parts], MOVES[4 + d]) for d in range(4)
        ]

    def deposit(weight):
        for y in range(CY):
            w = weight(y)
            values[0, rows_of(y), :] = w
            for c in range(3):
                values[1 + c, rows_of(y), :] = w * natural[c, rows_of(y), :]
        own = iota((CY, FLAT), 1) // CZ == iota((CY, FLAT), 0)
        out = [[] for _ in range(4)]
        for x in range(CX):
            picked = jnp.concatenate(
                [values[c, pl.ds(x, CY, stride=CX), :] for c in range(4)], axis=0
            )
            high, low = split(picked)
            both = dot_nt(jnp.concatenate([high, low], axis=0), deposit_hot[x])
            both = both[: 4 * CY] + both[4 * CY :]
            for c in range(4):
                part = jnp.where(own, both[c * CY : (c + 1) * CY], 0.0)
                out[c].append(jnp.sum(part, axis=0, keepdims=True))
        return [jnp.concatenate(o, axis=0) for o in out]

    def pack_x(parts, shift):
        at = iota((8, FLAT), 0) // 2
        out = jnp.zeros((8, FLAT), F32)
        for i, part in enumerate(parts):
            out = jnp.where(at == i, roll(part, 2 * i - shift, 0), out)
        return out

    def pack_y(parts, shift):
        at = iota((CX, 128), 1) // 32
        out = jnp.zeros((CX, 128), F32)
        for i, part in enumerate(parts):
            out = jnp.where(at == i, roll(part, 32 * i - shift, 1), out)
        return out

    def send_halo(step):
        own = [total[step, c] for c in range(4)]
        hx_out[step, 0, 0] = pack_x([w[8:16] for w in own], 6)
        hx_out[step, 1, 0] = pack_x([w[0:8] for w in own], 0)
        hy_out[step, 0, 0] = pack_y([w[:, 128:256] for w in own], 96)
        hy_out[step, 1, 0] = pack_y([w[:, 0:128] for w in own], 0)
        if step == 0:
            for d in range(4):
                counts = [count_ref[s * 8 + d].astype(F32) for s in range(STEPS)]
                if d < 2:
                    rows = slice(8, 16) if d == 0 else slice(0, 8)
                    packed = pack_x([fluid[rows], keep[rows]], 6 if d == 0 else 0)
                    at = iota((8, FLAT), 0)
                    packed = jnp.where(at == 4, counts[0], jnp.where(at == 5, counts[1], packed))
                    hx_out[0, d, 1] = packed
                else:
                    lanes = slice(128, 256) if d == 2 else slice(0, 128)
                    packed = pack_y([fluid[:, lanes], keep[:, lanes]], 96 if d == 2 else 0)
                    at = iota((CX, 128), 1) // 32
                    packed = jnp.where(at == 2, counts[0], jnp.where(at == 3, counts[1], packed))
                    hy_out[0, d - 2, 1] = packed
            return [
                send(hy_out.at[0, 0], hy.at[0, 0], MOVES[2]),
                send(hy_out.at[0, 1], hy.at[0, 1], MOVES[3]),
                send(hx_out.at[0, 0], hx.at[0, 0], MOVES[0]),
                send(hx_out.at[0, 1], hx.at[0, 1], MOVES[1]),
            ]
        return [
            send(hy_out.at[step, 0, 0], hy.at[step, 0, 0], MOVES[2]),
            send(hy_out.at[step, 1, 0], hy.at[step, 1, 0], MOVES[3]),
            send(hx_out.at[step, 0, 0], hx.at[step, 0, 0], MOVES[0]),
            send(hx_out.at[step, 1, 0], hx.at[step, 1, 0], MOVES[1]),
        ]

    def ring_x(own, low, high, i):
        at = iota((8, FLAT), 0)
        low = jnp.where((at >= 6) & present(MOVES[0]), roll(low, 6 - 2 * i, 0), 0.0)
        edge = jnp.where((at < 2) & present(MOVES[1]), roll(high, -2 * i, 0), low)
        return jnp.concatenate([own, edge], axis=0)

    def ring_y(own, low, high, i):
        at = iota((CX, 128), 1)
        low = jnp.where((at >= 96) & present(MOVES[2]), roll(low, 96 - 32 * i, 1), 0.0)
        edge = jnp.where((at < 32) & present(MOVES[3]), roll(high, -32 * i, 1), low)
        return jnp.concatenate([own, edge], axis=1)

    def move_x(w, k):
        return roll(w, -k, 0)

    def move_y(w, k):
        return roll(w, -k * CZ, 1)

    zpos = iota((CX, FLAT), 1) % CZ

    def move_z(w, k):
        inside = (zpos + k >= 0) & (zpos + k < CZ)
        return jnp.where(inside, roll(w, -k, 1), 0.0)

    def coefs():
        def one(f, k, move):
            return f * move(f, 1) * (1.0 - 0.5 * (k + move(k, 1)))

        ex = [(hx[0, 0, 1], hx[0, 1, 1], i) for i in range(2)]
        ey = [(hy[0, 0, 1], hy[0, 1, 1], i) for i in range(2)]
        x = one(ring_x(fluid, *ex[0]), ring_x(keep, *ex[1]), move_x)
        y = one(ring_y(fluid, *ey[0]), ring_y(keep, *ey[1]), move_y)
        return x, y, one(fluid, keep, move_z)

    def divergence(step, coef):
        own = [total[step, c] for c in range(4)]
        xs = [ring_x(own[c], hx[step, 0, 0], hx[step, 1, 0], c) for c in range(4)]
        ys = [ring_y(own[c], hy[step, 0, 0], hy[step, 1, 0], c) for c in range(4)]
        fx = flux_of(xs, coef[0], 0, move_x)
        fy = flux_of(ys, coef[1], 1, move_y)
        fz = flux_of(own, coef[2], 2, move_z)
        out = []
        for c in range(4):
            dx = (fx[c] - move_x(fx[c], -1))[:CX]
            dy = (fy[c] - move_y(fy[c], -1))[:, :FLAT]
            out.append(dx + dy + (fz[c] - move_z(fz[c], -1)))
        return out

    def collide(c, value):
        if c < 3:
            return value + COURANT * state[3 + c]
        if c == 6:
            return value * keep_turned[...]
        return 1.0 + (value - 1.0) * relax_turned[...]

    def fit_list(step):
        at = iota((1, CAP), 1).astype(F32)
        fits = []
        for d in range(4):
            if d < 2:
                count = hx[0, d, 1][4 + step : 5 + step, 0:1]
            else:
                count = hy[0, d - 2, 1][0:1, 64 + 32 * step : 65 + 32 * step]
            fits.append((at < jnp.broadcast_to(count, (1, CAP))) & present(MOVES[d]))
        lane = iota((4, 128), 1)
        got = jnp.zeros((4, 128), F32)
        for d in range(4):
            mine = (lane % 64) // DIAG == d
            got = jnp.where(mine & present(MOVES[4 + d]), diag_in[d, 0], got)
        flag = (roll(got, 64, 1) > 0.5) & (lane < 64)
        fits.append(flag[2 * step : 2 * step + 1])
        return jnp.concatenate([f.astype(F32) for f in fits], axis=1) > 0.5

    def arrived(fit, rows):
        lane = iota((4, 128), 1)
        corners = {}
        for part in sorted({part for part, _ in rows}):
            got = jnp.zeros((4, 128), F32)
            for d in range(4):
                mine = (lane % 64) // DIAG == d
                got = jnp.where(mine & present(MOVES[4 + d]), diag_in[d, part], got)
            corners[part] = got
        out = []
        for part, at in rows:
            pieces = [axial_in[d, part, at : at + 1, :] for d in range(4)]
            pieces.append(corners[part][at : at + 1])
            out.append(jnp.where(fit, jnp.concatenate(pieces, axis=1), 0.0))
        return out

    keep_turned[...] = turn(keep_slot)
    for c in (6, 3, 4, 5):
        load_state(c)
    weight = collide(6, state[6])
    state[6] = weight
    put_split(0, weight)
    for c in range(3):
        put_split(1 + c, state[3 + c])
    listed = [send_list(step) for step in range(STEPS)]
    axial_starts = list(range(0, AXIAL, 256))
    gather(listed[0], 0, [0], axial_starts + [AXIAL])
    flags = jnp.where(iota((8, 128), 0) < 2, listed[0][3], listed[1][3])
    flags = roll(flags, 64, 1)[0:4]
    diag_out[0] = jnp.where(iota((4, 128), 1) < 64, diag_out[0], flags)

    for x in range(CX):
        for y in range(CY):
            mine = iota((CZ, SLOTS), 0) == jnp.broadcast_to(
                cell_ref[x : x + 1, lanes_of(y)], (CZ, SLOTS)
            )
            deposit_hot[x, y * CZ : (y + 1) * CZ, :] = jnp.where(mine, 1.0, 0.0).astype(BF16)
    moments = deposit(lambda y: natural[3, rows_of(y), :])
    for copy in loads[8:]:
        copy.wait()
    fluid = pore_ref[...].astype(F32)
    for c in range(4):
        total[0, c] = (fields_ref[c] + moments[c]) * fluid
    pl.semaphore_wait(barrier, len(MOVES))
    first = send_corners(0, 1) + send_axial(0, 1)
    halo = send_halo(0)

    for copy in loads[6:8]:
        copy.wait()
    relax_turned[...] = turn(relax_slot)
    for k, c in enumerate((0, 1, 2, 7)):
        load_state(c)
        value = collide(c, state[c])
        put_split(9 + k, value)
        value = collide(c, value)
        put_split(5 + k, value)
        state[c] = value
    weight = collide(6, state[6])
    put_split(4, weight)
    state[6] = weight
    gather(listed[0], 9, [1], axial_starts + [AXIAL])
    gather(listed[1], 1, [2, 3], axial_starts + [AXIAL])
    late = send_corners(1, 3) + send_axial(1, 3)

    left = [
        dot_nt(onehot_rows(place, LIVE), row_hot) > 0.5 for _, place, row_hot, _ in listed
    ]
    gone = jnp.transpose(
        jnp.concatenate(
            [left[0].astype(F32), jnp.zeros((SLOTS - LIVE, BLOCKS), F32)], axis=0
        )
    )
    stay = deposit(
        lambda y: jnp.where(
            gone[rows_of(y)] > 0.5, 0.0, natural[3, rows_of(y), :] * keep_slot[y]
        )
    )
    slots = [slots_of(land_ref, step) for step in range(STEPS)]
    place_hots = [onehot_rows((t & 127) - DEAD, SPAN) for t in slots]
    row = block_row(slots[0])
    row_hots = [onehot_rows(block_row(t), BLOCKS) for t in slots]
    cell_all = turn([cell_ref[:, lanes_of(y)].astype(F32) for y in range(CY)])
    found = dot(cell_all[DEAD:].astype(BF16), row_hots[0])
    z = jnp.sum(
        jnp.where(iota((SPAN, LIST), 0) == (slots[0] & 127) - DEAD, found, 0.0),
        axis=0,
        keepdims=True,
    )
    flat_cell = (row >> 4).astype(F32) * CZ + z
    cell_hot = jnp.where(
        iota((FLAT, LIST), 0).astype(F32) == flat_cell, 1.0, 0.0
    ).astype(BF16)
    x_mine = iota((CX, LIST), 0) == (row & 15)
    table = jnp.concatenate([*split(keep), *split(relax)], axis=0)
    factors = dot(table, cell_hot)

    def factor(k):
        both = factors[2 * k * CX : (2 * k + 1) * CX] + factors[(2 * k + 1) * CX : (2 * k + 2) * CX]
        return jnp.sum(jnp.where(x_mine, both, 0.0), axis=0, keepdims=True)

    keep_land, relax_land = factor(0), factor(1)

    for copy in first + halo:
        copy.wait_recv()
    fit = [fit_list(step) for step in range(STEPS)]
    w, vx, vy, vz = arrived(fit[0], [(0, k) for k in range(4)])
    highs, lows = [], []
    for value in (w, w * vx, w * vy, w * vz):
        high, low = split(jnp.where(x_mine, value, 0.0))
        highs.append(high)
        lows.append(low)
    landed = dot_nt(jnp.concatenate(highs + lows, axis=0), cell_hot)
    landed = landed[: 4 * CX] + landed[4 * CX :]
    coef = coefs()
    div = divergence(0, coef)
    fields = [
        fields_ref[c] - COURANT * div[c] + (1.0 - keep) * moments[c] for c in range(4)
    ]
    moments = [stay[c] + landed[c * CX : (c + 1) * CX] for c in range(4)]
    for c in range(4):
        total[1, c] = (fields[c] + moments[c]) * fluid
    halo = send_halo(1)

    for c in range(8):
        rest = 1.0 - relax_turned[:LIVE] if c == 7 else 0.0
        value = jnp.where(left[0], rest, state[c, :LIVE])
        state[c, :LIVE] = jnp.where(left[1], 0.0, value)

    def land(step, comps, news):
        parts = []
        for new in news:
            high, low = split(new)
            parts += [place_hots[step] * high, place_hots[step] * low]
        if 7 in comps:
            parts.append(place_hots[step] * fit[step].astype(F32).astype(BF16))
        got = dot_nt(jnp.concatenate(parts, axis=0), row_hots[step])
        for i, c in enumerate(comps):
            new = got[2 * i * SPAN : (2 * i + 1) * SPAN]
            new = new + got[(2 * i + 1) * SPAN : (2 * i + 2) * SPAN]
            before = state[c, DEAD:]
            if c == 7:
                before = jnp.where(got[2 * len(comps) * SPAN :] > 0.5, 0.0, before)
            state[c, DEAD:] = before + new

    land(0, (6, 3, 4, 5), (w * keep_land, vx, vy, vz))
    for copy in late:
        copy.wait_recv()
    px, py, pz, rot = arrived(fit[0], [(1, k) for k in range(4)])
    land(
        0,
        (0, 1, 2, 7),
        (
            px + COURANT * vx,
            py + COURANT * vy,
            pz + COURANT * vz,
            jnp.where(fit[0], 1.0 + (rot - 1.0) * relax_land, 0.0),
        ),
    )
    land(
        1,
        (3, 4, 5, 6, 0, 1, 2, 7),
        arrived(fit[1], [(part, k) for part in (2, 3) for k in range(4)]),
    )
    for c in range(8):
        whole = jnp.transpose(state[c])
        for y in range(CY):
            part_out[c, :, lanes_of(y)] = whole[rows_of(y)]
    for copy in copies:
        copy.wait_send()
    for copy in halo:
        copy.wait_recv()
    div = divergence(1, coef)
    for c in range(4):
        fields_out[c] = fields[c] - COURANT * div[c] + (1.0 - keep) * moments[c]


def solution(mesh):
    nx, ny = mesh.shape["gx"], mesh.shape["gy"]

    def body(fields, pore, rate, particles, occupancy, slot_cell, send_slot, send_count, land_slot):
        vmem = pl.BlockSpec(memory_space=pltpu.VMEM)
        hbm = pl.BlockSpec(memory_space=pltpu.HBM)
        copies = 8 * STEPS + 8 + 4 * STEPS

        def run(*refs):
            kernel(nx, ny, *refs)

        results = pl.pallas_call(
            run,
            out_shape=(
                jax.ShapeDtypeStruct(fields.shape, F32),
                jax.ShapeDtypeStruct(particles.shape, F32),
            ),
            in_specs=[hbm] * 9,
            out_specs=(vmem, vmem),
            scratch_shapes=[
                pltpu.VMEM(fields.shape, F32),
                pltpu.VMEM(pore.shape, I32),
                pltpu.VMEM(rate.shape, F32),
                pltpu.VMEM(particles.shape, F32),
                pltpu.VMEM(occupancy.shape, I32),
                pltpu.VMEM(slot_cell.shape, I32),
                pltpu.VMEM(send_slot.shape, I32),
                pltpu.SMEM((STEPS * 8,), I32),
                pltpu.VMEM(land_slot.shape, I32),
                pltpu.SemaphoreType.DMA((11,)),
                pltpu.VMEM((8, SLOTS, BLOCKS), F32),
                pltpu.VMEM((4, BLOCKS, SLOTS), F32),
                pltpu.VMEM((SLOTS, BLOCKS), F32),
                pltpu.VMEM((SLOTS, BLOCKS), F32),
                pltpu.VMEM((13 * LIVE, 2 * BLOCKS), BF16),
                pltpu.VMEM((4, BLOCKS, SLOTS), F32),
                pltpu.VMEM((CX, FLAT, SLOTS), BF16),
                pltpu.VMEM((STEPS, 4, CX, FLAT), F32),
                pltpu.VMEM((STEPS, 2, 2, 8, FLAT), F32),
                pltpu.VMEM((STEPS, 2, 2, CX, 128), F32),
                pltpu.VMEM((STEPS, 2, 2, 8, FLAT), F32),
                pltpu.VMEM((STEPS, 2, 2, CX, 128), F32),
                pltpu.VMEM((4, 4, 4, CAP), F32),
                pltpu.VMEM((4, 4, 4, CAP), F32),
                pltpu.VMEM((4, 4, 128), F32),
                pltpu.VMEM((4, 4, 4, 128), F32),
                pltpu.SemaphoreType.DMA((copies,)),
                pltpu.SemaphoreType.DMA((copies,)),
            ],
            compiler_params=pltpu.CompilerParams(
                collective_id=0, has_side_effects=True, vmem_limit_bytes=48 << 20
            ),
        )(
            *[
                pltpu.with_memory_space_constraint(x, pltpu.HBM)
                for x in (
                    fields,
                    pore,
                    rate,
                    particles,
                    occupancy,
                    slot_cell,
                    send_slot,
                    send_count.reshape(STEPS * 8),
                    land_slot,
                )
            ]
        )

        def store(a, b, a_out, b_out, sem):
            both = [
                pltpu.make_async_copy(b, b_out, sem.at[0]),
                pltpu.make_async_copy(a, a_out, sem.at[1]),
            ]
            for copy in both:
                copy.start()
            for copy in both:
                copy.wait()

        return pl.pallas_call(
            store,
            out_shape=(
                jax.ShapeDtypeStruct(fields.shape, F32),
                jax.ShapeDtypeStruct(particles.shape, F32),
            ),
            in_specs=[vmem] * 2,
            out_specs=(hbm, hbm),
            scratch_shapes=[pltpu.SemaphoreType.DMA((2,))],
            compiler_params=pltpu.CompilerParams(vmem_limit_bytes=4 << 20),
        )(*results)

    return jax.shard_map(
        body,
        mesh=mesh,
        in_specs=(
            P(None, "gx", "gy"),
            P("gx", "gy"),
            P("gx", "gy"),
            P(None, "gx", "gy"),
            P("gx", "gy"),
            P("gx", "gy"),
            P(None, "gx", "gy"),
            P(None, "gx", "gy"),
            P(None, "gx", "gy"),
        ),
        out_specs=(P(None, "gx", "gy"), P(None, "gx", "gy")),
        check_vma=False,
    )
```
